32 devices in a mesh: blk: 8 (over z, x), dp: 4 (over y, core).
Axes of the slice: x: 2, y: 2, z: 4, core: 2. Of those that a mesh axis runs over, the one named last changes fastest.
Arguments:
- x_rows: bfloat16 [8192, 2048], P('blk'), may hold values from -6 to 6
- grad_rows: bfloat16 [8192, 2048], P('blk'), may hold values from -3 to 3
- w_gate_up: bfloat16 [8, 2, 768, 2048], P('blk', None, 'dp'), may hold values from -0.125 to 0.125
- w_down: bfloat16 [8, 768, 2048], P('blk', 'dp'), may hold values from -0.21875 to 0.21875
- counts: int32 [8, 5], replicated, may hold values from 1 to 384, as said below
Outputs:
- grad_gate_up: float32 [8, 2, 768, 2048], P('blk', None, 'dp')
- grad_down: float32 [8, 768, 2048], P('blk', 'dp')
- grad_x: bfloat16 [8192, 2048], P('blk', 'dp')
The draws below stay inside these ranges and needn't reach their ends.
Inputs may be any that keep to these rules, and one draw needn't show every extreme that they name: `counts`: on every device the 5 offsets take 3, 2, 1, 1 and 1 blocks of 128 rows, in an order drawn for each device, so the blocks fill all 1024 rows; an offset with k blocks has more than 128 * (k - 1) live rows; in every draw some device has an offset with exactly 384 live rows.
All inputs are finite; a program needn't handle non-finite values.
Results may differ from the reference program's by a relative error of at most 0.0095.
Values may be sent and summed in bfloat16 or wider, within the bound.
No kernel may reach another device: no remote copies, remote signals or barrier semaphores. Data moves between devices by JAX's collectives and lax.ppermute only.
A program may use at most 192 MiB of HBM per device.

```python
import jax
import jax.numpy as jnp
from jax import lax

D = 2048
FW = 768
BLOCK = 128
SPAN = 5
ROWS_DEV = 1024
EXPERTS = 8
N_BLK = 8
N_DP = 4


def draw_counts(key, part):
    subkeys = jax.random.split(jax.random.fold_in(key, 17), 3)
    orders = jax.vmap(lambda single: jax.random.permutation(single, SPAN))(jax.random.split(subkeys[0], N_BLK))
    rank_table = jnp.argsort(orders, axis=1, stable=True).astype(jnp.int32)
    block_table = jnp.array([3, 2] + [1] * (SPAN - 2), dtype=jnp.int32)
    blocks = block_table[rank_table]
    extra = jax.random.randint(subkeys[1], (N_BLK, SPAN), 0, BLOCK, dtype=jnp.int32)
    result = (blocks - 1) * BLOCK + 1 + extra
    chosen = jax.random.randint(subkeys[2], (), 0, N_BLK, dtype=jnp.int32)
    row_ids = jnp.arange(N_BLK, dtype=jnp.int32)[:, None]
    result = jnp.where((row_ids == chosen) & (blocks == 3), 3 * BLOCK, result)
    return result.astype(jnp.int32)


def level_of(stream_key, extent, pieces, smallest, largest):
    gain, own = 1.0, jax.random.fold_in(stream_key, 6)
    for position, parts in pieces:
        heights = jnp.exp(jax.random.uniform(jax.random.fold_in(own, position), (parts,), jnp.float32, smallest / len(pieces), largest / len(pieces)))
        gain = gain * jnp.repeat(heights, extent[position] // parts).reshape([-1 if axis == position else 1 for axis in range(len(extent))])
    return gain


def noise(own_key, dims, width, limit, shards=(), kind=jnp.bfloat16):
    values = width * jax.random.normal(own_key, dims, jnp.float32)
    if shards:
        values = values * level_of(own_key, dims, shards, -0.22, 0.18)
    return jnp.clip(values, -limit, limit).astype(kind)


def setup_inputs(seed: int = 0) -> dict:
    key_list = jax.random.split(jax.random.key(seed), 6)
    x_rows = noise(key_list[0], (N_BLK * ROWS_DEV, D), 1.0, 6.0, ((0, 8),))
    grad_rows = noise(key_list[1], (N_BLK * ROWS_DEV, D), 0.5, 3.0, ((0, 8),))
    w_gate_up = noise(key_list[2], (EXPERTS, 2, FW, D), D ** -0.5, 0.125, ((0, 8), (2, 4)))
    w_down = noise(key_list[3], (EXPERTS, FW, D), FW ** -0.5, 0.21875, ((0, 8), (1, 4)))
    counts = draw_counts(jax.random.fold_in(key_list[5], 71), 0)
    return dict(x_rows=x_rows, grad_rows=grad_rows, w_gate_up=w_gate_up, w_down=w_down, counts=counts)


def contract_last(lhs_array, rhs_array):
    return lax.dot_general(lhs_array, rhs_array, (((1,), (1,)), ((), ())), preferred_element_type=jnp.float32)


def contract_first(lhs_array, rhs_array):
    return lax.dot_general(lhs_array, rhs_array, (((0,), (0,)), ((), ())), preferred_element_type=jnp.float32)


def block_grads(weight_in, weight_out, rows_in, rows_cot):
    unit_count = weight_out.shape[0]
    projected = contract_last(rows_in, weight_in.reshape(2 * unit_count, weight_in.shape[2]))
    gate_pre = projected[:, :unit_count]
    up_pre = projected[:, unit_count:]
    sigmoid_gate = jax.nn.sigmoid(gate_pre)
    active = gate_pre * sigmoid_gate
    hidden = (active * up_pre).astype(jnp.bfloat16)
    hidden_grad = contract_last(rows_cot, weight_out)
    gate_gradient_rows = (hidden_grad * up_pre * sigmoid_gate * (1.0 + gate_pre * (1.0 - sigmoid_gate))).astype(jnp.bfloat16)
    up_gradient_rows = (hidden_grad * active).astype(jnp.bfloat16)
    grad_in = jnp.stack([contract_first(gate_gradient_rows, rows_in), contract_first(up_gradient_rows, rows_in)])
    grad_out = contract_first(hidden, rows_cot)
    row_grand_count = rows_in.shape[0]
    fourth_portion = unit_count // N_DP
    partial_value_sum = jnp.einsum("ewi,wip->ewp", gate_gradient_rows.reshape(row_grand_count, N_DP, fourth_portion).astype(jnp.float32),
                         weight_in[0].reshape(N_DP, fourth_portion, -1).astype(jnp.float32), precision=lax.Precision.HIGHEST)
    partial_value_sum = partial_value_sum + jnp.einsum("ewi,wip->ewp", up_gradient_rows.reshape(row_grand_count, N_DP, fourth_portion).astype(jnp.float32),
                                   weight_in[1].reshape(N_DP, fourth_portion, -1).astype(jnp.float32), precision=lax.Precision.HIGHEST)
    return grad_in, grad_out, partial_value_sum


def reference(x_rows, grad_rows, w_gate_up, w_down, counts):
    inputs_all = x_rows.reshape(N_BLK, ROWS_DEV, D)
    cotan_all = grad_rows.reshape(N_BLK, ROWS_DEV, D)

    def device_step(totals, packed):
        device, inputs, cotangent = packed
        own_counts = lax.dynamic_index_in_dim(counts, device, 0, keepdims=False).astype(jnp.int32)
        blocks = ((own_counts + BLOCK - 1) // BLOCK).astype(jnp.int32)
        block_limits = jnp.cumsum(blocks).astype(jnp.int32)
        starts = ((block_limits - blocks) * BLOCK).astype(jnp.int32)

        def block_step(running, block_idx):
            acc_in, acc_out = running
            offset = jnp.minimum(jnp.sum((block_limits <= block_idx).astype(jnp.int32)).astype(jnp.int32), SPAN - 1)
            row_first = (block_idx * BLOCK).astype(jnp.int32)
            local_row = row_first - starts[offset] + jnp.arange(BLOCK, dtype=jnp.int32)
            live_rows = local_row < own_counts[offset]
            rows_in = lax.dynamic_slice_in_dim(inputs, row_first, BLOCK, 0)
            rows_cot = lax.dynamic_slice_in_dim(cotangent, row_first, BLOCK, 0)
            rows_cot = jnp.where(live_rows[:, None], rows_cot, jnp.zeros((), rows_cot.dtype))
            expert = ((device - offset) % N_BLK).astype(jnp.int32)
            weight_in = lax.dynamic_index_in_dim(w_gate_up, expert, 0, keepdims=False)
            weight_out = lax.dynamic_index_in_dim(w_down, expert, 0, keepdims=False)
            grad_in, grad_out, partial_value_sum = block_grads(weight_in, weight_out, rows_in, rows_cot)
            acc_in = acc_in.at[expert].add(grad_in)
            acc_out = acc_out.at[expert].add(grad_out)
            return (acc_in, acc_out), partial_value_sum

        totals, partial_value_sum = lax.scan(block_step, totals, jnp.arange(ROWS_DEV // BLOCK, dtype=jnp.int32))
        partial_value_sum = partial_value_sum.reshape(ROWS_DEV, N_DP, D)
        rounded = lax.optimization_barrier(partial_value_sum.astype(jnp.bfloat16))
        result = jnp.sum(rounded.astype(jnp.float32), axis=1).astype(jnp.bfloat16)
        return totals, result

    start_in = jnp.zeros(w_gate_up.shape, jnp.float32)
    start_out = jnp.zeros(w_down.shape, jnp.float32)
    (grad_gate_up, grad_down), result = lax.scan(
        device_step, (start_in, start_out), (jnp.arange(N_BLK, dtype=jnp.int32), inputs_all, cotan_all))
    return grad_gate_up, grad_down, result.reshape(N_BLK * ROWS_DEV, D)
```

```python
import functools

import jax
import jax.numpy as jnp
from jax import lax
from jax.experimental import pallas as pl
from jax.experimental.pallas import tpu as pltpu
from jax.sharding import PartitionSpec as P

HOPS = 4
BLOCK = 128
MOST = 3
CHUNKS = 4


def shift(array, by):
    size = lax.axis_size("blk")
    return lax.ppermute(array, "blk", [((i + by) % size, i) for i in range(size)])


def swap_pair(array):
    return lax.ppermute(array, "blk", [(i, i ^ 1) for i in range(lax.axis_size("blk"))])


def swap_dp(array, bit):
    return lax.ppermute(array, "dp", [(i, i ^ bit) for i in range(lax.axis_size("dp"))])


def contract_last(lhs, rhs):
    return lax.dot_general(lhs, rhs, (((1,), (1,)), ((), ())), preferred_element_type=jnp.float32)


def matmul(lhs, rhs):
    return lax.dot_general(lhs, rhs, (((1,), (0,)), ((), ())), preferred_element_type=jnp.float32)


def grads(own, x_ref, c_ref, w_ref, v_ref, add_in, add_out, gate_s, up_s, hg_s, sum_in, sum_out, row_refs):
    depth = w_ref.shape[2]
    width = depth // CHUNKS

    def project(k, _):
        cols = pl.ds(pl.multiple_of(k * width, width), width)
        x = x_ref[:, cols]
        gate = contract_last(x, w_ref[0, :, cols])
        up = contract_last(x, w_ref[1, :, cols])
        hg = contract_last(c_ref[:, cols], v_ref[:, cols])

        @pl.when(k == 0)
        def _():
            gate_s[...] = gate
            up_s[...] = up
            hg_s[...] = hg

        @pl.when(k > 0)
        def _():
            gate_s[...] += gate
            up_s[...] += up
            hg_s[...] += hg

        return 0

    lax.fori_loop(0, CHUNKS, project, 0)
    gate_pre = gate_s[...]
    up_pre = up_s[...]
    hidden_grad = hg_s[...]
    sig = jax.nn.sigmoid(gate_pre)
    active = gate_pre * sig
    hidden = (active * up_pre).astype(jnp.bfloat16)
    gate_rows = (hidden_grad * up_pre * sig * (1.0 + gate_pre * (1.0 - sig))).astype(jnp.bfloat16)
    up_rows = (hidden_grad * active).astype(jnp.bfloat16)
    hidden_t = hidden.T
    gate_t = gate_rows.T
    up_t = up_rows.T

    def weights(k, _):
        cols = pl.ds(pl.multiple_of(k * width, width), width)
        x = x_ref[:, cols]
        in_gate = matmul(gate_t, x)
        in_up = matmul(up_t, x)
        out = matmul(hidden_t, c_ref[:, cols])
        if add_in is not None:
            in_gate += add_in[0, :, cols]
            in_up += add_in[1, :, cols]
            out += add_out[:, cols]
        sum_in[0, :, cols] = in_gate
        sum_in[1, :, cols] = in_up
        sum_out[:, cols] = out
        return 0

    lax.fori_loop(0, CHUNKS, weights, 0)
    for q, row_ref in enumerate(row_refs):
        cols = pl.ds(pl.multiple_of((own ^ q) * row_ref.shape[1], row_ref.shape[1]), row_ref.shape[1])
        row = matmul(gate_rows, w_ref[0, :, cols]) + matmul(up_rows, w_ref[1, :, cols])
        row_ref[...] = row.astype(jnp.bfloat16)


def home_kernel(s_ref, x_ref, c_ref, w_ref, v_ref, sum_in, sum_out, r0, r1, r2, r3, cot, gate_s, up_s, hg_s):
    rows = lax.broadcasted_iota(jnp.int32, (x_ref.shape[0], 1), 0)
    cot[...] = jnp.where(rows < s_ref[1], c_ref[...], jnp.zeros((), jnp.bfloat16))
    grads(s_ref[0], x_ref, cot, w_ref, v_ref, None, None, gate_s, up_s, hg_s, sum_in, sum_out, (r0, r1, r2, r3))


def away_kernel(s_ref, p0, p1, p2, p3, w_ref, v_ref, add_in, add_out,
                sum_in, sum_out, r0, r1, r2, r3, x_s, cot, gate_s, up_s, hg_s):
    own = s_ref[0]
    part = p0.shape[2]
    for t in range(p0.shape[0]):
        live = s_ref[1 + t] > 0
        for q, piece in enumerate((p0, p1, p2, p3)):
            at = pl.ds(pl.multiple_of(t * BLOCK + (own ^ q) * part, part), part)
            x_s[at, :] = piece[t, 0]
            cot[at, :] = jnp.where(live, piece[t, 1], jnp.zeros((), jnp.bfloat16))
    grads(own, x_s, cot, w_ref, v_ref, add_in, add_out, gate_s, up_s, hg_s, sum_in, sum_out, (r0, r1, r2, r3))


def estimate(rows, hidden, depth, parts):
    return pl.CostEstimate(
        flops=2 * rows * hidden * depth * 8,
        bytes_accessed=rows * depth * 6 + hidden * depth * (6 + 12 * parts),
        transcendentals=rows * hidden,
    )


def outputs(rows, hidden, depth):
    return [
        jax.ShapeDtypeStruct((2, hidden, depth), jnp.float32),
        jax.ShapeDtypeStruct((hidden, depth), jnp.float32),
    ] + [jax.ShapeDtypeStruct((rows, depth // 4), jnp.bfloat16)] * 4


def whole(shape):
    zeros = (0,) * len(shape)
    return pl.BlockSpec(shape, lambda i, s: zeros)


def process(kernel, scalars, rows, arrays, specs, hidden, depth, aliases, parts, scratch):
    outs = outputs(rows, hidden, depth)
    f32 = [pltpu.VMEM((rows, hidden), jnp.float32)] * 3
    return pl.pallas_call(
        kernel,
        out_shape=outs,
        grid_spec=pltpu.PrefetchScalarGridSpec(
            num_scalar_prefetch=1,
            grid=(1,),
            in_specs=specs,
            out_specs=[whole(o.shape) for o in outs],
            scratch_shapes=[pltpu.VMEM((rows, depth), jnp.bfloat16)] * scratch + f32,
        ),
        input_output_aliases=aliases,
        cost_estimate=estimate(rows, hidden, depth, parts),
    )(scalars, *arrays)


def merge_kernel(s_ref, *refs):
    *sources, out = refs
    n = out.shape[0]
    for b in range(n):
        for k, source in enumerate(sources):
            @pl.when(s_ref[0, b] == k)
            def _():
                out[b] = source[s_ref[1, b]]


def merge(pick, at, sources, n):
    sizes = jnp.array([s.shape[0] for s in sources], jnp.int32)
    at = jnp.clip(at, 0, sizes[pick] - 1)
    shape = (n,) + sources[0].shape[1:]
    return pl.pallas_call(
        merge_kernel,
        out_shape=jax.ShapeDtypeStruct(shape, sources[0].dtype),
        grid_spec=pltpu.PrefetchScalarGridSpec(
            num_scalar_prefetch=1,
            grid=(1,),
            in_specs=[whole(s.shape) for s in sources],
            out_specs=whole(shape),
        ),
    )(jnp.stack([pick, at]).astype(jnp.int32), *sources)


def gather_pieces(quarter):
    across = swap_dp(quarter, 2)
    return quarter, swap_dp(quarter, 1), across, swap_dp(across, 1)


def reduce_rows(parts):
    near, far = swap_dp(parts[1], 1), swap_dp(parts[3], 1)
    far = (parts[2].astype(jnp.float32) + far.astype(jnp.float32)).astype(jnp.bfloat16)
    far = swap_dp(far, 2)
    return (parts[0].astype(jnp.float32) + near.astype(jnp.float32) + far.astype(jnp.float32)).astype(jnp.bfloat16)


def on_device(x_rows, grad_rows, w_gate_up, w_down, counts):
    w_in, w_out = w_gate_up[0], w_down[0]
    hidden, depth = w_out.shape
    total = x_rows.shape[0]
    nblk = total // BLOCK
    n_dev = lax.axis_size("blk")
    n_dp = lax.axis_size("dp")
    assert n_dp == 4 and n_dev % 2 == 0 and n_dev > HOPS
    span = MOST * BLOCK
    part = BLOCK // n_dp
    me = lax.axis_index("blk")
    own = lax.axis_index("dp")
    odd = me % 2

    blocks = (counts + BLOCK - 1) // BLOCK
    starts = jnp.cumsum(blocks, axis=1) - blocks
    ahead = (me + jnp.arange(HOPS + 1)) % n_dev
    cnt = counts[ahead]
    nb = blocks[ahead]
    st = starts[ahead]
    window = jnp.minimum(st, nblk - MOST)
    ids = jnp.arange(nblk)
    offset_of = jnp.sum(ids[None, :, None] >= st[:, None, 1:], axis=2)
    spread = jnp.arange(MOST)
    diag = jnp.arange(HOPS + 1)
    w_diag = window[diag, diag]
    at = w_diag[:, None] + spread
    live = (at >= st[diag, diag][:, None]) & (at < (st + nb)[diag, diag][:, None])

    row = jnp.arange(total)
    row_offset = jnp.repeat(offset_of[0], BLOCK)
    alive = row - st[0][row_offset] * BLOCK < cnt[0][row_offset]
    pick = lambda a: lax.dynamic_index_in_dim(a.reshape(nblk, n_dp, part, -1), own, 1, keepdims=False)
    cot_q = jnp.where(pick(alive[:, None]), pick(grad_rows), jnp.zeros((), jnp.bfloat16))
    mine = jnp.stack([pick(x_rows), cot_q], axis=1)

    wide = shift(mine[3:], 2)
    narrow = shift(mine[1:3], 2)
    wider = shift(wide, 2)
    second = jnp.concatenate([narrow, wide])
    third = wider

    def cut(array, first, index):
        return lax.dynamic_slice_in_dim(array, index - first, MOST, 0)

    give_1 = jnp.where(odd == 1, cut(mine, 0, window[0, 1]), cut(second, 1, window[2, 1]))
    give_3 = jnp.where(odd == 1, cut(second, 1, window[2, 3]), cut(third, 3, jnp.maximum(window[4, 3], 3)))
    quarters = {
        1: swap_pair(give_1),
        2: cut(second, 1, window[2, 2]),
        3: swap_pair(give_3),
        4: cut(third, 3, jnp.maximum(window[4, 4], 3)),
    }

    rows_spec = whole((span, depth))
    weight_specs = [whole(w_in.shape), whole(w_out.shape)]
    base = jnp.stack([own, cnt[0, 0]]).astype(jnp.int32)
    sum_in, sum_out, *parts = process(
        home_kernel, base, span, (x_rows, grad_rows, w_in, w_out), [rows_spec, rows_spec] + weight_specs,
        hidden, depth, {}, 1, 1,
    )
    results = {0: reduce_rows(parts)}
    piece = (MOST, 2, part, depth)
    for o in (2, 1, 4, 3):
        scal = jnp.concatenate([own[None], live[o].astype(jnp.int32)]).astype(jnp.int32)
        pieces = gather_pieces(quarters[o])
        sum_in, sum_out, *parts = process(
            away_kernel, scal, span, (*pieces, w_in, w_out, sum_in, sum_out),
            [whole(piece)] * 4 + weight_specs + weight_specs, hidden, depth, {7: 0, 8: 1}, 2, 2,
        )
        results[o] = reduce_rows(parts)
    results = {o: r.reshape(MOST, BLOCK, -1) for o, r in results.items()}

    back_1 = swap_pair(results[1])
    back_3 = swap_pair(results[3])
    off = offset_of[4, 3:]
    ids_3 = ids[3:]
    is_3 = off <= 3
    far = merge(
        jnp.where(is_3, 0, 1),
        ids_3 - jnp.where(is_3, window[4, 3], window[4, 4]),
        [back_3, results[4]], nblk - 3,
    )
    far = shift(far, -2)
    off = offset_of[2, 1:]
    ids_1 = ids[1:]
    from_far = (off == 4) | ((off == 3) & (odd == 0))
    choice = jnp.where(from_far, 3, jnp.where(off == 3, 2, jnp.where(off == 2, 1, 0)))
    first = jnp.stack([window[2, 1], window[2, 2], window[2, 3], jnp.asarray(3, window.dtype)])
    near = merge(choice, ids_1 - first[choice], [back_1, results[2], back_3, far], nblk - 1)
    near = shift(near, -2)
    off = offset_of[0]
    choice = jnp.where(off == 0, 0, jnp.where((off == 1) & (odd == 1), 1, 2))
    first = jnp.stack([jnp.asarray(0, window.dtype), window[0, 1], jnp.asarray(1, window.dtype)])
    done = merge(choice, ids - first[choice], [results[0], back_1, near], nblk)
    return sum_in[None], sum_out[None], done.reshape(total, -1)


def solution(mesh):
    return jax.shard_map(
        on_device,
        mesh=mesh,
        in_specs=(
            P("blk", None),
            P("blk", None),
            P("blk", None, "dp", None),
            P("blk", "dp", None),
            P(),
        ),
        out_specs=(P("blk", None, "dp", None), P("blk", "dp", None), P("blk", "dp")),
        check_vma=False,
    )
```

```python
import functools

import jax
import jax.numpy as jnp
from jax import lax
from jax.experimental import pallas as pl
from jax.experimental.pallas import tpu as pltpu
from jax.sharding import PartitionSpec as P

HOPS = 4
SPAN = HOPS + 1
BLOCK = 128
MOST = 3
PARTS = 4
BF16 = jnp.bfloat16
F32 = jnp.float32


def size_of(axis):
    return lax.axis_size(axis)


def ahead(array, by, parity=None):
    size = size_of("blk")
    moves = lambda i: parity is None or i % 2 == parity
    return lax.ppermute(array, "blk", [((i + by) % size if moves(i) else i, i) for i in range(size)])


def swap_pair(array):
    return lax.ppermute(array, "blk", [(i, i ^ 1) for i in range(size_of("blk"))])


def swap_dp(array, bit):
    return lax.ppermute(array, "dp", [(i, i ^ bit) for i in range(size_of("dp"))])


def contract_last(lhs, rhs):
    return lax.dot_general(lhs, rhs, (((1,), (1,)), ((), ())), preferred_element_type=F32)


def matmul(lhs, rhs):
    return lax.dot_general(lhs, rhs, (((1,), (0,)), ((), ())), preferred_element_type=F32)


def whole(shape, **more):
    zeros = (0,) * len(shape)
    return pl.BlockSpec(tuple(shape), lambda i, s: zeros, **more)


OWN, ODD, WIN, START, LIM = 0, 1, 2, 2 + 2 * SPAN, 2 + 3 * SPAN
TABLE = LIM + SPAN * MOST


def table_kernel(n_dev, nblk, s_ref, out_ref):
    me, own = s_ref[0], s_ref[1]
    out_ref[OWN] = own
    out_ref[ODD] = lax.rem(me, 2)

    def count(device, o):
        return s_ref[2 + device * SPAN + o]

    def start(device, o):
        total = jnp.int32(0)
        for p in range(o):
            total += lax.div(count(device, p) + (BLOCK - 1), BLOCK)
        return total

    there = lax.rem(me + 2, n_dev)
    for o in range(SPAN):
        out_ref[START + o] = start(me, o)
        out_ref[WIN + o] = jnp.minimum(start(me, o), nblk - MOST)
        out_ref[WIN + SPAN + o] = jnp.minimum(start(there, o), nblk - MOST)
        device = lax.rem(me + o, n_dev)
        first = start(device, o)
        window = jnp.minimum(first, nblk - MOST)
        for t in range(MOST):
            block = window + t - first
            out_ref[LIM + o * MOST + t] = jnp.where(block >= 0, count(device, o) - block * BLOCK, 0)


def make_table(counts, n_dev, nblk):
    place = jnp.stack([lax.axis_index("blk"), lax.axis_index("dp")]).astype(jnp.int32)
    return pl.pallas_call(
        functools.partial(table_kernel, n_dev, nblk),
        out_shape=jax.ShapeDtypeStruct((TABLE,), jnp.int32),
        in_specs=[pl.BlockSpec(memory_space=pltpu.SMEM)],
        out_specs=pl.BlockSpec(memory_space=pltpu.SMEM),
    )(jnp.concatenate([place, counts.reshape(-1)]))


def cut_kernel(index, chosen, s_ref, *refs):
    *sources, out_ref = refs
    first = index(pl.program_id(0), s_ref)
    pairs = [sources[k : k + 2] for k in range(0, len(sources), 2)]
    for k, (low, high) in enumerate(pairs):
        for ref, here in ((low, first < 2), (high, first >= 2)):
            @pl.when(here & (chosen(s_ref) == k))
            def _():
                out_ref[...] = ref[...]


def cut(table, pairs, index, chosen=lambda s: 0):
    n_high = pairs[0][1].shape[0]
    block = (1,) + pairs[0][0].shape[1:]
    low = pl.BlockSpec(block, lambda t, s: (jnp.clip(index(t, s), 0, 1), 0, 0, 0))
    high = pl.BlockSpec(block, lambda t, s: (jnp.clip(index(t, s) - 2, 0, n_high - 1), 0, 0, 0))
    shape = (MOST,) + block[1:]
    return pl.pallas_call(
        functools.partial(cut_kernel, index, chosen),
        out_shape=jax.ShapeDtypeStruct(shape, BF16),
        grid_spec=pltpu.PrefetchScalarGridSpec(
            num_scalar_prefetch=1,
            grid=(MOST,),
            in_specs=[low, high] * len(pairs),
            out_specs=pl.BlockSpec(block, lambda t, s: (t, 0, 0, 0)),
        ),
    )(table, *[a for pair in pairs for a in pair])


def column(k, own):
    return (((k % 2) * 2) | (1 - k // 2)) ^ own


def expert_kernel(offsets, home, last, s_ref, *refs):
    refs = list(refs)
    take = lambda n: [refs.pop(0) for _ in range(n)]
    n_away = len(offsets) - home
    home_refs = take(2 * home)
    pieces = [take(2) for _ in range(n_away)]
    w_ref, v_ref = take(2)
    add_in, add_out = take(2) if last else (None, None)
    if last:
        own_in, own_out, far_in, far_out = take(4)
    else:
        sum_in, sum_out = take(2)
    give, keep, x_s, c_s, proj_s, hg_s, gu_s, gut_s, ht_s = refs
    step = pl.program_id(0)
    own = s_ref[OWN]
    core = own % 2
    half = BLOCK // 2
    quarter = BLOCK // PARTS
    depth = w_ref.shape[1]
    width = depth // PARTS
    units = v_ref.shape[0]

    @pl.when(step == 0)
    def _():
        def put(slot, t, at, size, x, c):
            rows = pl.ds(pl.multiple_of(slot * MOST * half + t * half + at, quarter), size)
            ids = lax.broadcasted_iota(jnp.int32, (size, 1), 0) + (own // 2) * half + at
            live = ids < s_ref[LIM + offsets[slot] * MOST + t]
            x_s[rows, :] = x
            c_s[rows, :] = jnp.where(live, c, jnp.zeros((), BF16))

        for slot in range(len(offsets)):
            for t in range(MOST):
                if slot < home:
                    put(slot, t, 0, half, home_refs[0][t, 0], home_refs[1][t, 0])
                else:
                    near, other = pieces[slot - home]
                    put(slot, t, core * quarter, quarter, near[t, 0], near[t, 1])
                    put(slot, t, (1 - core) * quarter, quarter, other[t, 0], other[t, 1])

        def project(k, _):
            cols = pl.ds(pl.multiple_of(k * width, width), width)
            proj = contract_last(x_s[:, cols], w_ref[:, cols])
            hg = contract_last(c_s[:, cols], v_ref[:, cols])

            @pl.when(k == 0)
            def _():
                proj_s[...] = proj
                hg_s[...] = hg

            @pl.when(k > 0)
            def _():
                proj_s[...] += proj
                hg_s[...] += hg

            return 0

        lax.fori_loop(0, PARTS, project, 0)
        gate_pre = proj_s[:, :units]
        up_pre = proj_s[:, units:]
        hidden_grad = hg_s[...]
        sig = jax.nn.sigmoid(gate_pre)
        active = gate_pre * sig
        hidden = (active * up_pre).astype(BF16)
        gate_rows = (hidden_grad * up_pre * sig * (1.0 + gate_pre * (1.0 - sig))).astype(BF16)
        up_rows = (hidden_grad * active).astype(BF16)
        gu_s[:, :units] = gate_rows
        gu_s[:, units:] = up_rows
        gut_s[:units, :] = gate_rows.T
        gut_s[units:, :] = up_rows.T
        ht_s[...] = hidden.T

    cols = pl.ds(pl.multiple_of(column(step, own) * width, width), width)
    new_in = matmul(gut_s[...], x_s[:, cols])
    new_out = matmul(ht_s[...], c_s[:, cols])
    if last:
        new_in += add_in[...]
        new_out += add_out[...]
        fw = units // 2
        own_in[0] = new_in[:fw]
        own_in[1] = new_in[units : units + fw]
        own_out[...] = new_out[:fw]
        far_in[0] = new_in[fw:units].astype(BF16)
        far_in[1] = new_in[units + fw :].astype(BF16)
        far_out[...] = new_out[fw:].astype(BF16)
    else:
        sum_in[...] = new_in
        sum_out[...] = new_out
    row_grad = matmul(gu_s[...], w_ref[:, cols]).astype(BF16)

    @pl.when(step < 2)
    def _():
        give[0] = row_grad

    @pl.when(step >= 2)
    def _():
        keep[0] = row_grad


def expert(table, offsets, home, pieces, w_all, v_all, sums):
    last = sums is not None
    depth = w_all.shape[1]
    units = v_all.shape[0]
    fw = units // 2
    width = depth // PARTS
    half = BLOCK // 2
    rows = len(offsets) * MOST * half
    once = pl.Buffered(1)
    arrays, specs = [], []
    for a in home:
        arrays.append(a.reshape(-1, 2, half, depth))
        specs.append(pl.BlockSpec((MOST, 1, half, depth), lambda i, s: (0, s[OWN] // 2, 0, 0), pipeline_mode=once))
    for pair in pieces:
        for a in pair:
            arrays.append(a)
            specs.append(whole(a.shape, pipeline_mode=once))
    for a in (w_all, v_all):
        arrays.append(a)
        specs.append(whole(a.shape, pipeline_mode=once))
    chunk_in = pl.BlockSpec((2 * units, width), lambda i, s: (0, column(i, s[OWN])))
    chunk_out = pl.BlockSpec((units, width), lambda i, s: (0, column(i, s[OWN])))
    own_in = pl.BlockSpec((2, fw, width), lambda i, s: (0, 0, column(i, s[OWN])))
    own_out = pl.BlockSpec((fw, width), lambda i, s: (0, column(i, s[OWN])))
    if last:
        arrays += list(sums)
        specs += [chunk_in, chunk_out]
        shapes = [((2, fw, depth), F32), ((fw, depth), F32), ((2, fw, depth), BF16), ((fw, depth), BF16)]
        outs = [own_in, own_out, own_in, own_out]
    else:
        shapes = [((2 * units, depth), F32), ((units, depth), F32)]
        outs = [chunk_in, chunk_out]
    shapes += [((2, rows, width), BF16)] * 2
    outs += [
        pl.BlockSpec((1, rows, width), lambda i, s: (jnp.minimum(i, 1), 0, 0)),
        pl.BlockSpec((1, rows, width), lambda i, s: (jnp.maximum(i - 2, 0), 0, 0)),
    ]
    return pl.pallas_call(
        functools.partial(expert_kernel, tuple(offsets), len(home) // 2, last),
        out_shape=[jax.ShapeDtypeStruct(*s) for s in shapes],
        grid_spec=pltpu.PrefetchScalarGridSpec(
            num_scalar_prefetch=1,
            grid=(PARTS,),
            in_specs=specs,
            out_specs=outs,
            scratch_shapes=[
                pltpu.VMEM((rows, depth), BF16),
                pltpu.VMEM((rows, depth), BF16),
                pltpu.VMEM((rows, 2 * units), F32),
                pltpu.VMEM((rows, units), F32),
                pltpu.VMEM((rows, 2 * units), BF16),
                pltpu.VMEM((2 * units, rows), BF16),
                pltpu.VMEM((units, rows), BF16),
            ],
        ),
        cost_estimate=pl.CostEstimate(
            flops=16 * rows * units * depth,
            bytes_accessed=rows * depth * 6 + units * depth * (6 + (24 if last else 12)),
            transcendentals=rows * units,
        ),
    )(table, *arrays)


def row_sums(give, keep, n):
    got = swap_dp(give, 1)
    shape = (2, n, MOST, BLOCK // 2, keep.shape[-1])
    both = (keep.astype(F32) + got.astype(F32)).astype(BF16).reshape(shape)
    other = swap_dp(both[1], 2)
    return [jnp.stack([both[0, k], other[k]]) for k in range(n)]


def merge_kernel(s_ref, *refs):
    *sources, out = refs
    half = BLOCK // 2
    y = s_ref[OWN] // 2
    for b in range(out.shape[0]):
        for o, source in enumerate(sources):
            begin = s_ref[START + o]
            end = s_ref[START + o + 1] if o + 1 < SPAN else out.shape[0]

            @pl.when((b >= begin) & (b < end))
            def _():
                at = jnp.clip(b - s_ref[WIN + o], 0, MOST - 1)
                out[b, pl.ds(pl.multiple_of(y * half, half), half), :] = source[0, at]
                out[b, pl.ds(pl.multiple_of((1 - y) * half, half), half), :] = source[1, at]


def merge(table, sources, nblk):
    shape = (nblk, BLOCK, sources[0].shape[-1])
    return pl.pallas_call(
        merge_kernel,
        out_shape=jax.ShapeDtypeStruct(shape, BF16),
        grid_spec=pltpu.PrefetchScalarGridSpec(
            num_scalar_prefetch=1,
            grid=(1,),
            in_specs=[whole(s.shape) for s in sources],
            out_specs=whole(shape),
        ),
    )(table, *sources)


def on_device(x_rows, grad_rows, w_gate_up, w_down, counts):
    w_in, w_out = w_gate_up[0], w_down[0]
    hidden, depth = w_out.shape
    total = x_rows.shape[0]
    nblk = total // BLOCK
    n_dev = size_of("blk")
    assert size_of("dp") == PARTS and n_dev % 2 == 0 and n_dev > HOPS
    part = BLOCK // PARTS
    own = lax.axis_index("dp")

    def pick(array, first, end):
        array = array.reshape(nblk, PARTS, part, depth)
        return lax.dynamic_slice(array, (first, own, 0, 0), (end - first, 1, part, depth))

    def quarter(first, end):
        return jnp.concatenate([pick(x_rows, first, end), pick(grad_rows, first, end)], axis=1)

    o_in, o_out = swap_dp(w_in, 2), swap_dp(w_out, 2)
    my_wide = quarter(3, nblk)
    wide = ahead(my_wide, 2)
    my_wide, counts, x_rows, grad_rows = lax.optimization_barrier((my_wide, counts, x_rows, grad_rows))
    my_narrow = quarter(1, 3)
    narrow = ahead(my_narrow, 2)
    table = make_table(counts, n_dev, nblk)

    fourth = ahead(wide[nblk - 3 - MOST :], 2)
    third = swap_pair(lax.dynamic_slice_in_dim(wide, table[WIN + SPAN + 3] - 3, MOST, 0))
    third = ahead(third, 2, parity=1)
    second = cut(table, [(narrow, wide)], lambda t, s: s[WIN + SPAN + 2] - 1 + t)
    first = cut(
        table,
        [(narrow, wide), (my_narrow, my_wide)],
        lambda t, s: jnp.where(s[ODD] == 1, s[WIN + 1], s[WIN + SPAN + 1]) - 1 + t,
        lambda s: s[ODD],
    )
    first = swap_pair(first)

    w_all = jnp.concatenate([w_in[0], o_in[0], w_in[1], o_in[1]])
    v_all = jnp.concatenate([w_out, o_out])
    pair = lambda a: (a, swap_dp(a, 1))
    sum_in, sum_out, give, keep = expert(
        table, (0, 2, 4), (x_rows, grad_rows), [pair(second), pair(fourth)], w_all, v_all, None
    )
    r0, r2, r4 = row_sums(give, keep, 3)
    own_in, own_out, far_in, far_out, give, keep = expert(
        table, (1, 3), (), [pair(first), pair(third)], w_all, v_all, (sum_in, sum_out)
    )
    r1, r3 = row_sums(give, keep, 2)
    far_in, far_out = swap_dp(far_in, 2), swap_dp(far_out, 2)
    r2 = ahead(r2, -2)
    r4 = ahead(ahead(r4, -2), -2)
    r1 = ahead(swap_pair(r1), -2, parity=0)
    r3 = ahead(swap_pair(ahead(r3, -2, parity=1)), -2)
    done = merge(table, [r0, r1, r2, r3, r4], nblk)
    return (own_in + far_in)[None], (own_out + far_out)[None], done.reshape(total, -1)


def solution(mesh):
    return jax.shard_map(
        on_device,
        mesh=mesh,
        in_specs=(
            P("blk", None),
            P("blk", None),
            P("blk", None, "dp", None),
            P("blk", "dp", None),
            P(),
        ),
        out_specs=(P("blk", None, "dp", None), P("blk", "dp", None), P("blk", "dp")),
        check_vma=False,
    )
```

```python
import functools

import jax
import jax.numpy as jnp
from jax import lax
from jax.experimental import pallas as pl
from jax.experimental.pallas import tpu as pltpu
from jax.sharding import PartitionSpec as P

HOPS = 4
SPAN = HOPS + 1
BLOCK = 128
MOST = 3
PARTS = 4
BF16 = jnp.bfloat16
F32 = jnp.float32


def size_of(axis):
    return lax.axis_size(axis)


def ahead(array, by, parity=None):
    size = size_of("blk")
    moves = lambda i: parity is None or i % 2 == parity
    return lax.ppermute(array, "blk", [((i + by) % size if moves(i) else i, i) for i in range(size)])


def swap_pair(array):
    return lax.ppermute(array, "blk", [(i, i ^ 1) for i in range(size_of("blk"))])


def swap_dp(array, bit):
    return lax.ppermute(array, "dp", [(i, i ^ bit) for i in range(size_of("dp"))])


def contract_last(lhs, rhs):
    return lax.dot_general(lhs, rhs, (((1,), (1,)), ((), ())), preferred_element_type=F32)


def matmul(lhs, rhs):
    return lax.dot_general(lhs, rhs, (((1,), (0,)), ((), ())), preferred_element_type=F32)


def whole(shape, **more):
    zeros = (0,) * len(shape)
    return pl.BlockSpec(tuple(shape), lambda i, s: zeros, **more)


OWN, ODD, WIN, START, LIM = 0, 1, 2, 2 + 2 * SPAN, 2 + 3 * SPAN
TABLE = LIM + SPAN * MOST


def table_kernel(n_dev, nblk, s_ref, out_ref):
    me, own = s_ref[0], s_ref[1]
    out_ref[OWN] = own
    out_ref[ODD] = lax.rem(me, 2)

    def count(device, o):
        return s_ref[2 + device * SPAN + o]

    def start(device, o):
        total = jnp.int32(0)
        for p in range(o):
            total += lax.div(count(device, p) + (BLOCK - 1), BLOCK)
        return total

    there = lax.rem(me + 2, n_dev)
    for o in range(SPAN):
        out_ref[START + o] = start(me, o)
        out_ref[WIN + o] = jnp.minimum(start(me, o), nblk - MOST)
        out_ref[WIN + SPAN + o] = jnp.minimum(start(there, o), nblk - MOST)
        device = lax.rem(me + o, n_dev)
        first = start(device, o)
        window = jnp.minimum(first, nblk - MOST)
        for t in range(MOST):
            block = window + t - first
            out_ref[LIM + o * MOST + t] = jnp.where(block >= 0, count(device, o) - block * BLOCK, 0)


def make_table(counts, n_dev, nblk):
    place = jnp.stack([lax.axis_index("blk"), lax.axis_index("dp")]).astype(jnp.int32)
    return pl.pallas_call(
        functools.partial(table_kernel, n_dev, nblk),
        out_shape=jax.ShapeDtypeStruct((TABLE,), jnp.int32),
        in_specs=[pl.BlockSpec(memory_space=pltpu.SMEM)],
        out_specs=pl.BlockSpec(memory_space=pltpu.SMEM),
    )(jnp.concatenate([place, counts.reshape(-1)]))


def cut_kernel(chosen, s_ref, *refs):
    *sources, out_ref = refs
    for k, source in enumerate(sources):
        @pl.when(chosen(s_ref) == k)
        def _():
            out_ref[...] = source[...]


def cut(table, sources, index, chosen=lambda s: 0):
    n = sources[0].shape[0]
    block = (1,) + sources[0].shape[1:]
    return pl.pallas_call(
        functools.partial(cut_kernel, chosen),
        out_shape=jax.ShapeDtypeStruct((MOST,) + block[1:], BF16),
        grid_spec=pltpu.PrefetchScalarGridSpec(
            num_scalar_prefetch=1,
            grid=(MOST,),
            in_specs=[pl.BlockSpec(block, lambda t, s: (jnp.clip(index(s) + t, 0, n - 1), 0, 0, 0))] * len(sources),
            out_specs=pl.BlockSpec(block, lambda t, s: (t, 0, 0, 0)),
        ),
    )(table, *sources)


def column(k, own):
    return (((k % 2) * 2) | (1 - k // 2)) ^ own


def expert_kernel(offsets, home, last, s_ref, *refs):
    refs = list(refs)
    take = lambda n: [refs.pop(0) for _ in range(n)]
    n_away = len(offsets) - home
    home_refs = take(2 * home)
    pieces = [take(2) for _ in range(n_away)]
    shares = take(4)
    add_in, add_out = take(2) if last else (None, None)
    if last:
        own_in, own_out, far_in, far_out = take(4)
    else:
        sum_in, sum_out = take(2)
    give, keep, w_ref, v_ref, sems, x_s, c_s, proj_s, hg_s, gu_s, gut_s, ht_s = refs
    step = pl.program_id(0)
    own = s_ref[OWN]
    core = own % 2
    half = BLOCK // 2
    quarter = BLOCK // PARTS
    depth = w_ref.shape[1]
    width = depth // PARTS
    units = v_ref.shape[0]
    fw = units // 2

    @pl.when(step == 0)
    def _():
        copies = []
        for k in range(2):
            w_share, v_share = shares[2 * k : 2 * k + 2]
            for g in range(2):
                copies.append((w_share.at[g], w_ref.at[pl.ds(g * units + k * fw, fw)]))
            copies.append((v_share, v_ref.at[pl.ds(k * fw, fw)]))
        copies = [pltpu.make_async_copy(a, b, sems.at[n]) for n, (a, b) in enumerate(copies)]
        for copy in copies:
            copy.start()

        def put(slot, t, at, size, x, c):
            rows = pl.ds(pl.multiple_of(slot * MOST * half + t * half + at, quarter), size)
            ids = lax.broadcasted_iota(jnp.int32, (size, 1), 0) + (own // 2) * half + at
            live = ids < s_ref[LIM + offsets[slot] * MOST + t]
            x_s[rows, :] = x
            c_s[rows, :] = jnp.where(live, c, jnp.zeros((), BF16))

        for slot in range(len(offsets)):
            for t in range(MOST):
                if slot < home:
                    put(slot, t, 0, half, home_refs[0][t, 0], home_refs[1][t, 0])
                else:
                    near, other = pieces[slot - home]
                    put(slot, t, core * quarter, quarter, near[t, 0], near[t, 1])
                    put(slot, t, (1 - core) * quarter, quarter, other[t, 0], other[t, 1])

        for copy in copies:
            copy.wait()

        def project(k, _):
            cols = pl.ds(pl.multiple_of(k * width, width), width)
            proj = contract_last(x_s[:, cols], w_ref[:, cols])
            hg = contract_last(c_s[:, cols], v_ref[:, cols])

            @pl.when(k == 0)
            def _():
                proj_s[...] = proj
                hg_s[...] = hg

            @pl.when(k > 0)
            def _():
                proj_s[...] += proj
                hg_s[...] += hg

            return 0

        lax.fori_loop(0, PARTS, project, 0)
        gate_pre = proj_s[:, :units]
        up_pre = proj_s[:, units:]
        hidden_grad = hg_s[...]
        sig = jax.nn.sigmoid(gate_pre)
        active = gate_pre * sig
        hidden = (active * up_pre).astype(BF16)
        gate_rows = (hidden_grad * up_pre * sig * (1.0 + gate_pre * (1.0 - sig))).astype(BF16)
        up_rows = (hidden_grad * active).astype(BF16)
        gu_s[:, :units] = gate_rows
        gu_s[:, units:] = up_rows
        gut_s[:units, :] = gate_rows.T
        gut_s[units:, :] = up_rows.T
        ht_s[...] = hidden.T

    cols = pl.ds(pl.multiple_of(column(step, own) * width, width), width)
    new_in = matmul(gut_s[...], x_s[:, cols])
    new_out = matmul(ht_s[...], c_s[:, cols])
    if last:
        new_in += add_in[...]
        new_out += add_out[...]
        own_in[0] = new_in[:fw]
        own_in[1] = new_in[units : units + fw]
        own_out[...] = new_out[:fw]
        far_in[0] = new_in[fw:units].astype(BF16)
        far_in[1] = new_in[units + fw :].astype(BF16)
        far_out[...] = new_out[fw:].astype(BF16)
    else:
        sum_in[...] = new_in
        sum_out[...] = new_out
    row_grad = matmul(gu_s[...], w_ref[:, cols]).astype(BF16)

    @pl.when(step < 2)
    def _():
        give[0] = row_grad

    @pl.when(step >= 2)
    def _():
        keep[0] = row_grad


def expert(table, offsets, home, pieces, shares, sums):
    last = sums is not None
    fw, depth = shares[1].shape
    units = 2 * fw
    width = depth // PARTS
    half = BLOCK // 2
    rows = len(offsets) * MOST * half
    once = pl.Buffered(1)
    arrays, specs = [], []
    for a in home:
        arrays.append(a.reshape(-1, 2, half, depth))
        specs.append(pl.BlockSpec((MOST, 1, half, depth), lambda i, s: (0, s[OWN] // 2, 0, 0), pipeline_mode=once))
    for pair in pieces:
        for a in pair:
            arrays.append(a)
            specs.append(whole(a.shape, pipeline_mode=once))
    for a in shares:
        arrays.append(a)
        specs.append(pl.BlockSpec(memory_space=pl.ANY))
    chunk_in = pl.BlockSpec((2 * units, width), lambda i, s: (0, column(i, s[OWN])))
    chunk_out = pl.BlockSpec((units, width), lambda i, s: (0, column(i, s[OWN])))
    own_in = pl.BlockSpec((2, fw, width), lambda i, s: (0, 0, column(i, s[OWN])))
    own_out = pl.BlockSpec((fw, width), lambda i, s: (0, column(i, s[OWN])))
    if last:
        arrays += list(sums)
        specs += [chunk_in, chunk_out]
        shapes = [((2, fw, depth), F32), ((fw, depth), F32), ((2, fw, depth), BF16), ((fw, depth), BF16)]
        outs = [own_in, own_out, own_in, own_out]
    else:
        shapes = [((2 * units, depth), F32), ((units, depth), F32)]
        outs = [chunk_in, chunk_out]
    shapes += [((2, rows, width), BF16)] * 2
    outs += [
        pl.BlockSpec((1, rows, width), lambda i, s: (jnp.minimum(i, 1), 0, 0)),
        pl.BlockSpec((1, rows, width), lambda i, s: (jnp.maximum(i - 2, 0), 0, 0)),
    ]
    return pl.pallas_call(
        functools.partial(expert_kernel, tuple(offsets), len(home) // 2, last),
        out_shape=[jax.ShapeDtypeStruct(*s) for s in shapes],
        grid_spec=pltpu.PrefetchScalarGridSpec(
            num_scalar_prefetch=1,
            grid=(PARTS,),
            in_specs=specs,
            out_specs=outs,
            scratch_shapes=[
                pltpu.VMEM((2 * units, depth), BF16),
                pltpu.VMEM((units, depth), BF16),
                pltpu.SemaphoreType.DMA((6,)),
                pltpu.VMEM((rows, depth), BF16),
                pltpu.VMEM((rows, depth), BF16),
                pltpu.VMEM((rows, 2 * units), F32),
                pltpu.VMEM((rows, units), F32),
                pltpu.VMEM((rows, 2 * units), BF16),
                pltpu.VMEM((2 * units, rows), BF16),
                pltpu.VMEM((units, rows), BF16),
            ],
        ),
        compiler_params=pltpu.CompilerParams(vmem_limit_bytes=30 * 2**20),
        cost_estimate=pl.CostEstimate(
            flops=16 * rows * units * depth,
            bytes_accessed=rows * depth * 6 + units * depth * (6 + (24 if last else 12)),
            transcendentals=rows * units,
        ),
    )(table, *arrays)


def add_cores(give, keep, n):
    got = swap_dp(give, 1)
    shape = (n, MOST, BLOCK // 2, keep.shape[-1])
    return [(keep[k].astype(F32) + got[k].astype(F32)).astype(BF16).reshape(shape) for k in range(2)]


def add_rows(here, other):
    return [jnp.stack([here[k], other[k]]) for k in range(other.shape[0])]


def merge_kernel(s_ref, *refs):
    *sources, out = refs
    half = BLOCK // 2
    y = s_ref[OWN] // 2
    for b in range(out.shape[0]):
        for o, source in enumerate(sources):
            begin = s_ref[START + o]
            end = s_ref[START + o + 1] if o + 1 < SPAN else out.shape[0]

            @pl.when((b >= begin) & (b < end))
            def _():
                at = jnp.clip(b - s_ref[WIN + o], 0, MOST - 1)
                out[b, pl.ds(pl.multiple_of(y * half, half), half), :] = source[0, at]
                out[b, pl.ds(pl.multiple_of((1 - y) * half, half), half), :] = source[1, at]


def merge(table, sources, nblk):
    shape = (nblk, BLOCK, sources[0].shape[-1])
    return pl.pallas_call(
        merge_kernel,
        out_shape=jax.ShapeDtypeStruct(shape, BF16),
        grid_spec=pltpu.PrefetchScalarGridSpec(
            num_scalar_prefetch=1,
            grid=(1,),
            in_specs=[whole(s.shape) for s in sources],
            out_specs=whole(shape),
        ),
    )(table, *sources)


def on_device(x_rows, grad_rows, w_gate_up, w_down, counts):
    w_in, w_out = w_gate_up[0], w_down[0]
    hidden, depth = w_out.shape
    total = x_rows.shape[0]
    nblk = total // BLOCK
    n_dev = size_of("blk")
    assert size_of("dp") == PARTS and n_dev % 2 == 0 and n_dev > HOPS
    part = BLOCK // PARTS
    own = lax.axis_index("dp")

    def pick(array, first, end):
        array = array.reshape(nblk, PARTS, part, depth)
        return lax.dynamic_slice(array, (first, own, 0, 0), (end - first, 1, part, depth))

    def quarter(first, end):
        return jnp.concatenate([pick(x_rows, first, end), pick(grad_rows, first, end)], axis=1)

    mine = quarter(1, nblk)
    there = ahead(mine, 2)
    o_in, o_out = swap_dp(w_in, 2), swap_dp(w_out, 2)
    mine, counts = lax.optimization_barrier((mine, counts))
    table = make_table(counts, n_dev, nblk)

    fourth = ahead(there[nblk - 1 - MOST :], 2)
    third = cut(table, [there], lambda s: s[WIN + SPAN + 3] - 1)
    third, there = lax.optimization_barrier((third, there))
    first = cut(
        table, [there, mine],
        lambda s: jnp.where(s[ODD] == 1, s[WIN + 1], s[WIN + SPAN + 1]) - 1, lambda s: s[ODD],
    )
    third = ahead(swap_pair(third), 2, parity=1)
    first, there = lax.optimization_barrier((first, there))
    second = cut(table, [there], lambda s: s[WIN + SPAN + 2] - 1)
    first = swap_pair(first)
    shares = (w_in, w_out, o_in, o_out)
    pair = lambda a: (a, swap_dp(a, 1))
    sum_in, sum_out, give, keep = expert(
        table, (0, 2, 4), (x_rows, grad_rows), [pair(second), pair(fourth)], shares, None
    )
    here, there = add_cores(give, keep, 3)
    sum_in, there = lax.optimization_barrier((sum_in, there))
    r0, r2, r4 = add_rows(here, swap_dp(there, 2))
    own_in, own_out, far_in, far_out, give, keep = expert(
        table, (1, 3), (), [pair(first), pair(third)], shares, (sum_in, sum_out)
    )
    here, there = add_cores(give, keep, 2)
    there = swap_dp(there, 2)
    there, far_in, far_out = lax.optimization_barrier((there, far_in, far_out))
    r1, r3 = add_rows(here, there)
    far_in, far_out = swap_dp(far_in, 2), swap_dp(far_out, 2)
    results = [r0] + [ahead(r, -o) for o, r in ((1, r1), (2, r2), (3, r3), (4, r4))]
    done = merge(table, results, nblk)
    return (own_in + far_in)[None], (own_out + far_out)[None], done.reshape(total, -1)


def solution(mesh):
    return jax.shard_map(
        on_device,
        mesh=mesh,
        in_specs=(
            P("blk", None),
            P("blk", None),
            P("blk", None, "dp", None),
            P("blk", "dp", None),
            P(),
        ),
        out_specs=(P("blk", None, "dp", None), P("blk", "dp", None), P("blk", "dp")),
        check_vma=False,
    )
```

```python
import functools

import jax
import jax.numpy as jnp
from jax import lax
from jax.experimental import pallas as pl
from jax.experimental.pallas import tpu as pltpu
from jax.sharding import PartitionSpec as P


HOPS = 4
SPAN = HOPS + 1
BLOCK = 128
MOST = 3
PARTS = 4
BF16 = jnp.bfloat16
F32 = jnp.float32


def size_of(axis):
    return lax.axis_size(axis)


def ahead(array, by, parity=None):
    size = size_of("blk")
    moves = lambda i: parity is None or i % 2 == parity
    return lax.ppermute(array, "blk", [((i + by) % size if moves(i) else i, i) for i in range(size)])


def swap_pair(array):
    return lax.ppermute(array, "blk", [(i, i ^ 1) for i in range(size_of("blk"))])


def swap_dp(array, bit):
    return lax.ppermute(array, "dp", [(i, i ^ bit) for i in range(size_of("dp"))])


def contract_last(lhs, rhs):
    return lax.dot_general(lhs, rhs, (((1,), (1,)), ((), ())), preferred_element_type=F32)


def matmul(lhs, rhs):
    return lax.dot_general(lhs, rhs, (((1,), (0,)), ((), ())), preferred_element_type=F32)


def whole(shape, **more):
    zeros = (0,) * len(shape)
    return pl.BlockSpec(tuple(shape), lambda i, s: zeros, **more)


OWN, ODD, WIN, START, LIM = 0, 1, 2, 2 + 2 * SPAN, 2 + 3 * SPAN
TABLE = LIM + SPAN * MOST


def table_kernel(n_dev, nblk, s_ref, out_ref):
    me, own = s_ref[0], s_ref[1]
    out_ref[OWN] = own
    out_ref[ODD] = lax.rem(me, 2)

    def count(device, o):
        return s_ref[2 + device * SPAN + o]

    def start(device, o):
        total = jnp.int32(0)
        for p in range(o):
            total += lax.div(count(device, p) + (BLOCK - 1), BLOCK)
        return total

    there = lax.rem(me + 2, n_dev)
    for o in range(SPAN):
        out_ref[START + o] = start(me, o)
        out_ref[WIN + o] = jnp.minimum(start(me, o), nblk - MOST)
        out_ref[WIN + SPAN + o] = jnp.minimum(start(there, o), nblk - MOST)
        device = lax.rem(me + o, n_dev)
        first = start(device, o)
        window = jnp.minimum(first, nblk - MOST)
        for t in range(MOST):
            block = window + t - first
            out_ref[LIM + o * MOST + t] = jnp.where(block >= 0, count(device, o) - block * BLOCK, 0)


def make_table(counts, n_dev, nblk):
    place = jnp.stack([lax.axis_index("blk"), lax.axis_index("dp")]).astype(jnp.int32)
    return pl.pallas_call(
        functools.partial(table_kernel, n_dev, nblk),
        out_shape=jax.ShapeDtypeStruct((TABLE,), jnp.int32),
        in_specs=[pl.BlockSpec(memory_space=pltpu.SMEM)],
        out_specs=pl.BlockSpec(memory_space=pltpu.SMEM),
    )(jnp.concatenate([place, counts.reshape(-1)]))


def cut(array, index):
    return lax.dynamic_slice_in_dim(array, index, MOST, 0)


def column(k, own):
    return (((k % 2) * 2) | (1 - k // 2)) ^ own


def expert_kernel(offsets, home, last, s_ref, *refs):
    refs = list(refs)
    take = lambda n: [refs.pop(0) for _ in range(n)]
    n_away = len(offsets) - home
    home_refs = take(2 * home)
    pieces = [take(2) for _ in range(n_away)]
    shares = take(4)
    add_in, add_out = take(2) if last else (None, None)
    if last:
        own_in, own_out, far_in, far_out = take(4)
    else:
        sum_in, sum_out = take(2)
    give, keep, w_ref, v_ref, sems, x_s, c_s, proj_s, hg_s, gu_s, gut_s, ht_s = refs
    step = pl.program_id(0)
    own = s_ref[OWN]
    core = own % 2
    half = BLOCK // 2
    quarter = BLOCK // PARTS
    depth = w_ref.shape[1]
    width = depth // PARTS
    units = v_ref.shape[0]
    fw = units // 2

    @pl.when(step == 0)
    def _():
        copies = []
        for k in range(2):
            w_share, v_share = shares[2 * k : 2 * k + 2]
            for g in range(2):
                copies.append((w_share.at[g], w_ref.at[pl.ds(g * units + k * fw, fw)]))
            copies.append((v_share, v_ref.at[pl.ds(k * fw, fw)]))
        copies = [pltpu.make_async_copy(a, b, sems.at[n]) for n, (a, b) in enumerate(copies)]
        for copy in copies:
            copy.start()

        def put(slot, t, at, size, x, c):
            rows = pl.ds(pl.multiple_of(slot * MOST * half + t * half + at, quarter), size)
            ids = lax.broadcasted_iota(jnp.int32, (size, 1), 0) + (own // 2) * half + at
            live = ids < s_ref[LIM + offsets[slot] * MOST + t]
            x_s[rows, :] = x
            c_s[rows, :] = jnp.where(live, c, jnp.zeros((), BF16))

        for slot in range(len(offsets)):
            for t in range(MOST):
                if slot < home:
                    put(slot, t, 0, half, home_refs[0][t, 0], home_refs[1][t, 0])
                else:
                    near, other = pieces[slot - home]
                    put(slot, t, core * quarter, quarter, near[t, 0], near[t, 1])
                    put(slot, t, (1 - core) * quarter, quarter, other[t, 0], other[t, 1])

        for copy in copies:
            copy.wait()

        def project(k, _):
            cols = pl.ds(pl.multiple_of(k * width, width), width)
            proj = contract_last(x_s[:, cols], w_ref[:, cols])
            hg = contract_last(c_s[:, cols], v_ref[:, cols])

            @pl.when(k == 0)
            def _():
                proj_s[...] = proj
                hg_s[...] = hg

            @pl.when(k > 0)
            def _():
                proj_s[...] += proj
                hg_s[...] += hg

            return 0

        lax.fori_loop(0, PARTS, project, 0)
        gate_pre = proj_s[:, :units]
        up_pre = proj_s[:, units:]
        hidden_grad = hg_s[...]
        sig = jax.nn.sigmoid(gate_pre)
        active = gate_pre * sig
        hidden = (active * up_pre).astype(BF16)
        gate_rows = (hidden_grad * up_pre * sig * (1.0 + gate_pre * (1.0 - sig))).astype(BF16)
        up_rows = (hidden_grad * active).astype(BF16)
        gu_s[:, :units] = gate_rows
        gu_s[:, units:] = up_rows
        gut_s[:units, :] = gate_rows.T
        gut_s[units:, :] = up_rows.T
        ht_s[...] = hidden.T

    cols = pl.ds(pl.multiple_of(column(step, own) * width, width), width)
    new_in = matmul(gut_s[...], x_s[:, cols])
    new_out = matmul(ht_s[...], c_s[:, cols])
    if last:
        new_in += add_in[...]
        new_out += add_out[...]
        own_in[0] = new_in[:fw]
        own_in[1] = new_in[units : units + fw]
        own_out[...] = new_out[:fw]
        far_in[0] = new_in[fw:units].astype(BF16)
        far_in[1] = new_in[units + fw :].astype(BF16)
        far_out[...] = new_out[fw:].astype(BF16)
    else:
        sum_in[...] = new_in
        sum_out[...] = new_out
    row_grad = matmul(gu_s[...], w_ref[:, cols]).astype(BF16)

    @pl.when(step < 2)
    def _():
        give[0] = row_grad

    @pl.when(step >= 2)
    def _():
        keep[0] = row_grad


def expert(table, offsets, home, pieces, shares, sums):
    last = sums is not None
    fw, depth = shares[1].shape
    units = 2 * fw
    width = depth // PARTS
    half = BLOCK // 2
    rows = len(offsets) * MOST * half
    once = pl.Buffered(1)
    arrays, specs = [], []
    for a in home:
        arrays.append(a)
        specs.append(whole(a.shape, pipeline_mode=once))
    for pair in pieces:
        for a in pair:
            arrays.append(a)
            specs.append(whole(a.shape, pipeline_mode=once))
    for a in shares:
        arrays.append(a)
        specs.append(pl.BlockSpec(memory_space=pl.ANY))
    chunk_in = pl.BlockSpec((2 * units, width), lambda i, s: (0, column(i, s[OWN])))
    chunk_out = pl.BlockSpec((units, width), lambda i, s: (0, column(i, s[OWN])))
    own_in = pl.BlockSpec((2, fw, width), lambda i, s: (0, 0, column(i, s[OWN])))
    own_out = pl.BlockSpec((fw, width), lambda i, s: (0, column(i, s[OWN])))
    if last:
        arrays += list(sums)
        specs += [chunk_in, chunk_out]
        shapes = [((2, fw, depth), F32), ((fw, depth), F32), ((2, fw, depth), BF16), ((fw, depth), BF16)]
        outs = [own_in, own_out, own_in, own_out]
    else:
        shapes = [((2 * units, depth), F32), ((units, depth), F32)]
        outs = [chunk_in, chunk_out]
    shapes += [((2, rows, width), BF16)] * 2
    outs += [
        pl.BlockSpec((1, rows, width), lambda i, s: (jnp.minimum(i, 1), 0, 0)),
        pl.BlockSpec((1, rows, width), lambda i, s: (jnp.maximum(i - 2, 0), 0, 0)),
    ]
    return pl.pallas_call(
        functools.partial(expert_kernel, tuple(offsets), len(home) // 2, last),
        out_shape=[jax.ShapeDtypeStruct(*s) for s in shapes],
        grid_spec=pltpu.PrefetchScalarGridSpec(
            num_scalar_prefetch=1,
            grid=(PARTS,),
            in_specs=specs,
            out_specs=outs,
            scratch_shapes=[
                pltpu.VMEM((2 * units, depth), BF16),
                pltpu.VMEM((units, depth), BF16),
                pltpu.SemaphoreType.DMA((6,)),
                pltpu.VMEM((rows, depth), BF16),
                pltpu.VMEM((rows, depth), BF16),
                pltpu.VMEM((rows, 2 * units), F32),
                pltpu.VMEM((rows, units), F32),
                pltpu.VMEM((rows, 2 * units), BF16),
                pltpu.VMEM((2 * units, rows), BF16),
                pltpu.VMEM((units, rows), BF16),
            ],
        ),
        compiler_params=pltpu.CompilerParams(vmem_limit_bytes=28 * 2**20),
        cost_estimate=pl.CostEstimate(
            flops=16 * rows * units * depth,
            bytes_accessed=rows * depth * 6 + units * depth * (6 + (24 if last else 12)),
            transcendentals=rows * units,
        ),
    )(table, *arrays)


def add_cores(give, keep, n):
    got = swap_dp(give, 1)
    shape = (n, MOST, BLOCK // 2, keep.shape[-1])
    return [(keep[k].astype(F32) + got[k].astype(F32)).astype(BF16).reshape(shape) for k in range(2)]


def add_rows(here, other):
    return [jnp.stack([here[k], other[k]]) for k in range(other.shape[0])]


def merge_kernel(s_ref, *refs):
    *sources, out = refs
    half = BLOCK // 2
    y = s_ref[OWN] // 2
    for b in range(out.shape[0]):
        for o, source in enumerate(sources):
            begin = s_ref[START + o]
            end = s_ref[START + o + 1] if o + 1 < SPAN else out.shape[0]

            @pl.when((b >= begin) & (b < end))
            def _():
                at = jnp.clip(b - s_ref[WIN + o], 0, MOST - 1)
                out[b, pl.ds(pl.multiple_of(y * half, half), half), :] = source[0, at]
                out[b, pl.ds(pl.multiple_of((1 - y) * half, half), half), :] = source[1, at]


def merge(table, sources, nblk):
    shape = (nblk, BLOCK, sources[0].shape[-1])
    return pl.pallas_call(
        merge_kernel,
        out_shape=jax.ShapeDtypeStruct(shape, BF16),
        grid_spec=pltpu.PrefetchScalarGridSpec(
            num_scalar_prefetch=1,
            grid=(1,),
            in_specs=[whole(s.shape) for s in sources],
            out_specs=whole(shape),
        ),
    )(table, *sources)


def on_device(x_rows, grad_rows, w_gate_up, w_down, counts):
    w_in, w_out = w_gate_up[0], w_down[0]
    _, depth = w_out.shape
    total = x_rows.shape[0]
    nblk = total // BLOCK
    n_dev = size_of("blk")
    assert size_of("dp") == PARTS and n_dev % 2 == 0 and n_dev > HOPS
    part = BLOCK // PARTS
    own = lax.axis_index("dp")

    def pick(array, first, end):
        array = array.reshape(nblk, PARTS, part, depth)
        return lax.dynamic_slice(array, (first, own, 0, 0), (end - first, 1, part, depth))

    def quarter(first, end):
        return jnp.concatenate([pick(x_rows, first, end), pick(grad_rows, first, end)], axis=1)

    mine = quarter(1, nblk)
    there = ahead(mine, 2)
    mine, counts, x_rows, grad_rows = lax.optimization_barrier((mine, counts, x_rows, grad_rows))
    table = make_table(counts, n_dev, nblk)
    o_in, o_out = swap_dp(w_in, 2), swap_dp(w_out, 2)
    home = lambda a: lax.dynamic_slice(
        a[: MOST * BLOCK].reshape(MOST, 2, BLOCK // 2, depth), (0, own // 2, 0, 0), (MOST, 1, BLOCK // 2, depth)
    )

    fourth = ahead(there[nblk - 1 - MOST :], 2)
    third = swap_pair(cut(there, table[WIN + SPAN + 3] - 1))
    third = ahead(third, 2, parity=1)
    first = jnp.where(table[ODD] == 1, cut(mine, table[WIN + 1] - 1), cut(there, table[WIN + SPAN + 1] - 1))
    first = swap_pair(first)
    second = cut(there, table[WIN + SPAN + 2] - 1)
    shares = (w_in, w_out, o_in, o_out)
    pair = lambda a: (a, swap_dp(a, 1))
    sum_in, sum_out, give, keep = expert(
        table, (0, 2, 4), (home(x_rows), home(grad_rows)), [pair(second), pair(fourth)], shares, None
    )
    here, there = add_cores(give, keep, 3)
    sum_in, there = lax.optimization_barrier((sum_in, there))
    there = swap_dp(there, 2)
    r0, r2, r4 = add_rows(here, there)
    pieces = [pair(first), pair(third)]
    own_in, own_out, far_in, far_out, give, keep = expert(table, (1, 3), (), pieces, shares, (sum_in, sum_out))
    here, there = add_cores(give, keep, 2)
    there = swap_dp(there, 2)
    there, far_in, far_out = lax.optimization_barrier((there, far_in, far_out))
    r1, r3 = add_rows(here, there)
    far_in, far_out = swap_dp(far_in, 2), swap_dp(far_out, 2)
    results = [r0] + [ahead(r, -o) for o, r in ((1, r1), (2, r2), (3, r3), (4, r4))]
    done = merge(table, results, nblk)
    return (own_in + far_in)[None], (own_out + far_out)[None], done.reshape(total, -1)


def solution(mesh):
    return jax.shard_map(
        on_device,
        mesh=mesh,
        in_specs=(
            P("blk", None),
            P("blk", None),
            P("blk", None, "dp", None),
            P("blk", "dp", None),
            P(),
        ),
        out_specs=(P("blk", None, "dp", None), P("blk", "dp", None), P("blk", "dp")),
        check_vma=False,
    )
```

```python
import functools

import jax
import jax.numpy as jnp
from jax import lax
from jax.experimental import pallas as pl
from jax.experimental.pallas import tpu as pltpu
from jax.sharding import PartitionSpec as P


HOPS = 4
SPAN = HOPS + 1
BLOCK = 128
MOST = 3
PARTS = 4
BF16 = jnp.bfloat16
F32 = jnp.float32


def size_of(axis):
    return lax.axis_size(axis)


def ahead(array, by, parity=None):
    size = size_of("blk")
    moves = lambda i: parity is None or i % 2 == parity
    return lax.ppermute(array, "blk", [((i + by) % size if moves(i) else i, i) for i in range(size)])


def swap_pair(array):
    return lax.ppermute(array, "blk", [(i, i ^ 1) for i in range(size_of("blk"))])


def swap_dp(array, bit):
    return lax.ppermute(array, "dp", [(i, i ^ bit) for i in range(size_of("dp"))])


def contract_last(lhs, rhs):
    return lax.dot_general(lhs, rhs, (((1,), (1,)), ((), ())), preferred_element_type=F32)


def matmul(lhs, rhs):
    return lax.dot_general(lhs, rhs, (((1,), (0,)), ((), ())), preferred_element_type=F32)


def whole(shape, **more):
    zeros = (0,) * len(shape)
    return pl.BlockSpec(tuple(shape), lambda i, s: zeros, **more)


OWN, ODD, WIN, START, LIM = 0, 1, 2, 2 + 2 * SPAN, 2 + 3 * SPAN
TABLE = LIM + SPAN * MOST


def table_kernel(n_dev, nblk, s_ref, out_ref):
    me, own = s_ref[0], s_ref[1]
    out_ref[OWN] = own
    out_ref[ODD] = lax.rem(me, 2)

    def count(device, o):
        return s_ref[2 + device * SPAN + o]

    def start(device, o):
        total = jnp.int32(0)
        for p in range(o):
            total += lax.div(count(device, p) + (BLOCK - 1), BLOCK)
        return total

    there = lax.rem(me + 2, n_dev)
    for o in range(SPAN):
        out_ref[START + o] = start(me, o)
        out_ref[WIN + o] = jnp.minimum(start(me, o), nblk - MOST)
        out_ref[WIN + SPAN + o] = jnp.minimum(start(there, o), nblk - MOST)
        device = lax.rem(me + o, n_dev)
        first = start(device, o)
        window = jnp.minimum(first, nblk - MOST)
        for t in range(MOST):
            block = window + t - first
            out_ref[LIM + o * MOST + t] = jnp.where(block >= 0, count(device, o) - block * BLOCK, 0)


def make_table(counts, n_dev, nblk):
    place = jnp.stack([lax.axis_index("blk"), lax.axis_index("dp")]).astype(jnp.int32)
    return pl.pallas_call(
        functools.partial(table_kernel, n_dev, nblk),
        out_shape=jax.ShapeDtypeStruct((TABLE,), jnp.int32),
        in_specs=[pl.BlockSpec(memory_space=pltpu.SMEM)],
        out_specs=pl.BlockSpec(memory_space=pltpu.SMEM),
    )(jnp.concatenate([place, counts.reshape(-1)]))


def cut(array, index):
    return lax.dynamic_slice_in_dim(array, index, MOST, 0)


def column(k, own):
    return (((k % 2) * 2) | (1 - k // 2)) ^ own


def expert_kernel(offsets, home, last, s_ref, *refs):
    refs = list(refs)
    take = lambda n: [refs.pop(0) for _ in range(n)]
    n_away = len(offsets) - home
    home_refs = take(2 * home)
    pieces = [take(2) for _ in range(n_away)]
    shares = take(4)
    add_in, add_out = take(2) if last else (None, None)
    if last:
        own_in, own_out, far_in, far_out = take(4)
    else:
        sum_in, sum_out = take(2)
    give, keep, w_ref, v_ref, sems, x_s, c_s, proj_s, hg_s, gu_s, gut_s, ht_s = refs
    step = pl.program_id(0)
    own = s_ref[OWN]
    core = own % 2
    half = BLOCK // 2
    quarter = BLOCK // PARTS
    depth = w_ref.shape[1]
    width = depth // PARTS
    units = v_ref.shape[0]
    fw = units // 2

    @pl.when(step == 0)
    def _():
        moves = []
        for k in range(2):
            w_share, v_share = shares[2 * k : 2 * k + 2]
            for g in range(2):
                moves.append((w_share.at[g], w_ref.at[pl.ds(g * units + k * fw, fw)]))
            moves.append((v_share, v_ref.at[pl.ds(k * fw, fw)]))
        for slot in range(len(offsets)):
            for t in range(MOST):
                base = (slot * MOST + t) * half
                if slot < home:
                    for ref, rows in zip(home_refs, (x_s, c_s)):
                        moves.append((ref.at[t, 0], rows.at[pl.ds(base, half)]))
                else:
                    for ref, at in zip(pieces[slot - home], (core, 1 - core)):
                        place = pl.ds(pl.multiple_of(base + at * quarter, quarter), quarter)
                        for g, rows in enumerate((x_s, c_s)):
                            moves.append((ref.at[t, g], rows.at[place]))
        copies = [pltpu.make_async_copy(a, b, sems.at[n]) for n, (a, b) in enumerate(moves)]
        for copy in copies:
            copy.start()
        for copy in copies:
            copy.wait()
        for slot in range(len(offsets)):
            for t in range(MOST):
                limit = s_ref[LIM + offsets[slot] * MOST + t]
                rows = pl.ds((slot * MOST + t) * half, half)

                @pl.when(limit < BLOCK)
                def _():
                    ids = lax.broadcasted_iota(jnp.int32, (half, 1), 0) + (own // 2) * half
                    c_s[rows, :] = jnp.where(ids < limit, c_s[rows, :], jnp.zeros((), BF16))

        proj_s[...] = contract_last(x_s[...], w_ref[...])
        hg_s[...] = contract_last(c_s[...], v_ref[...])
        gate_pre = proj_s[:, :units]
        up_pre = proj_s[:, units:]
        hidden_grad = hg_s[...]
        sig = jax.nn.sigmoid(gate_pre)
        active = gate_pre * sig
        hidden = (active * up_pre).astype(BF16)
        gate_rows = (hidden_grad * up_pre * sig * (1.0 + gate_pre * (1.0 - sig))).astype(BF16)
        up_rows = (hidden_grad * active).astype(BF16)
        gu_s[:, :units] = gate_rows
        gu_s[:, units:] = up_rows
        gut_s[:units, :] = gate_rows.T
        gut_s[units:, :] = up_rows.T
        ht_s[...] = hidden.T

    cols = pl.ds(pl.multiple_of(column(step, own) * width, width), width)
    new_in = matmul(gut_s[...], x_s[:, cols])
    new_out = matmul(ht_s[...], c_s[:, cols])
    if last:
        new_in += add_in[...]
        new_out += add_out[...]
        own_in[0] = new_in[:fw]
        own_in[1] = new_in[units : units + fw]
        own_out[...] = new_out[:fw]
        far_in[0] = new_in[fw:units].astype(BF16)
        far_in[1] = new_in[units + fw :].astype(BF16)
        far_out[...] = new_out[fw:].astype(BF16)
    else:
        sum_in[...] = new_in
        sum_out[...] = new_out
    row_grad = matmul(gu_s[...], w_ref[:, cols]).astype(BF16)

    @pl.when(step < 2)
    def _():
        give[0] = row_grad

    @pl.when(step >= 2)
    def _():
        keep[0] = row_grad


def expert(table, offsets, home, pieces, shares, sums):
    last = sums is not None
    fw, depth = shares[1].shape
    units = 2 * fw
    width = depth // PARTS
    half = BLOCK // 2
    rows = len(offsets) * MOST * half
    arrays, specs = [], []
    for a in home:
        arrays.append(a)
        specs.append(pl.BlockSpec(memory_space=pl.ANY))
    for pair in pieces:
        for a in pair:
            arrays.append(a)
            specs.append(pl.BlockSpec(memory_space=pl.ANY))
    for a in shares:
        arrays.append(a)
        specs.append(pl.BlockSpec(memory_space=pl.ANY))
    chunk_in = pl.BlockSpec((2 * units, width), lambda i, s: (0, column(i, s[OWN])))
    chunk_out = pl.BlockSpec((units, width), lambda i, s: (0, column(i, s[OWN])))
    own_in = pl.BlockSpec((2, fw, width), lambda i, s: (0, 0, column(i, s[OWN])))
    own_out = pl.BlockSpec((fw, width), lambda i, s: (0, column(i, s[OWN])))
    if last:
        arrays += list(sums)
        specs += [chunk_in, chunk_out]
        shapes = [((2, fw, depth), F32), ((fw, depth), F32), ((2, fw, depth), BF16), ((fw, depth), BF16)]
        outs = [own_in, own_out, own_in, own_out]
    else:
        shapes = [((2 * units, depth), F32), ((units, depth), F32)]
        outs = [chunk_in, chunk_out]
    shapes += [((2, rows, width), BF16)] * 2
    outs += [
        pl.BlockSpec((1, rows, width), lambda i, s: (jnp.minimum(i, 1), 0, 0)),
        pl.BlockSpec((1, rows, width), lambda i, s: (jnp.maximum(i - 2, 0), 0, 0)),
    ]
    return pl.pallas_call(
        functools.partial(expert_kernel, tuple(offsets), len(home) // 2, last),
        out_shape=[jax.ShapeDtypeStruct(*s) for s in shapes],
        grid_spec=pltpu.PrefetchScalarGridSpec(
            num_scalar_prefetch=1,
            grid=(PARTS,),
            in_specs=specs,
            out_specs=outs,
            scratch_shapes=[
                pltpu.VMEM((2 * units, depth), BF16),
                pltpu.VMEM((units, depth), BF16),
                pltpu.SemaphoreType.DMA((6 + MOST * (len(home) + 4 * len(pieces)),)),
                pltpu.VMEM((rows, depth), BF16),
                pltpu.VMEM((rows, depth), BF16),
                pltpu.VMEM((rows, 2 * units), F32),
                pltpu.VMEM((rows, units), F32),
                pltpu.VMEM((rows, 2 * units), BF16),
                pltpu.VMEM((2 * units, rows), BF16),
                pltpu.VMEM((units, rows), BF16),
            ],
        ),
        compiler_params=pltpu.CompilerParams(vmem_limit_bytes=25 * 2**20),
        cost_estimate=pl.CostEstimate(
            flops=16 * rows * units * depth,
            bytes_accessed=rows * depth * 6 + units * depth * (6 + (24 if last else 12)),
            transcendentals=rows * units,
        ),
    )(table, *arrays)


def add_cores(give, keep, n):
    got = swap_dp(give, 1)
    shape = (n, MOST, BLOCK // 2, keep.shape[-1])
    return [(keep[k].astype(F32) + got[k].astype(F32)).astype(BF16).reshape(shape) for k in range(2)]


def add_rows(here, other):
    return [jnp.stack([here[k], other[k]]) for k in range(other.shape[0])]


def merge_kernel(s_ref, *refs):
    *sources, out = refs
    half = BLOCK // 2
    y = s_ref[OWN] // 2
    for b in range(out.shape[0]):
        for o, source in enumerate(sources):
            begin = s_ref[START + o]
            end = s_ref[START + o + 1] if o + 1 < SPAN else out.shape[0]

            @pl.when((b >= begin) & (b < end))
            def _():
                at = jnp.clip(b - s_ref[WIN + o], 0, MOST - 1)
                out[b, pl.ds(pl.multiple_of(y * half, half), half), :] = source[0, at]
                out[b, pl.ds(pl.multiple_of((1 - y) * half, half), half), :] = source[1, at]


def merge(table, sources, nblk):
    shape = (nblk, BLOCK, sources[0].shape[-1])
    return pl.pallas_call(
        merge_kernel,
        out_shape=jax.ShapeDtypeStruct(shape, BF16),
        grid_spec=pltpu.PrefetchScalarGridSpec(
            num_scalar_prefetch=1,
            grid=(1,),
            in_specs=[whole(s.shape) for s in sources],
            out_specs=whole(shape),
        ),
    )(table, *sources)


def on_device(x_rows, grad_rows, w_gate_up, w_down, counts):
    w_in, w_out = w_gate_up[0], w_down[0]
    _, depth = w_out.shape
    total = x_rows.shape[0]
    nblk = total // BLOCK
    n_dev = size_of("blk")
    assert size_of("dp") == PARTS and n_dev % 2 == 0 and n_dev > HOPS
    part = BLOCK // PARTS
    own = lax.axis_index("dp")

    def pick(array, first, end):
        array = array.reshape(nblk, PARTS, part, depth)
        return lax.dynamic_slice(array, (first, own, 0, 0), (end - first, 1, part, depth))

    def quarter(first, end):
        return jnp.concatenate([pick(x_rows, first, end), pick(grad_rows, first, end)], axis=1)

    mine = quarter(1, nblk)
    there = ahead(mine, 2)
    mine, counts, x_rows, grad_rows = lax.optimization_barrier((mine, counts, x_rows, grad_rows))
    table = make_table(counts, n_dev, nblk)
    home = [
        lax.dynamic_slice(a.reshape(nblk, 2, -1, depth), (0, own // 2, 0, 0), (MOST, 1, BLOCK // 2, depth))
        for a in (x_rows, grad_rows)
    ]
    o_in, o_out = swap_dp(w_in, 2), swap_dp(w_out, 2)

    third = cut(there, table[WIN + SPAN + 3] - 1)
    first = jnp.where(table[ODD] == 1, cut(mine, table[WIN + 1] - 1), cut(there, table[WIN + SPAN + 1] - 1))
    second = cut(there, table[WIN + SPAN + 2] - 1)
    fourth = there[nblk - 1 - MOST :]
    third = ahead(third, 1)
    first = swap_pair(first)
    fourth = ahead(fourth, 2)

    def pair(a):
        return a, swap_dp(a, 1)

    shares = (w_in, w_out, o_in, o_out)
    pieces = [pair(second), pair(third)]
    sum_in, sum_out, give, keep = expert(table, (0, 2, 3), home, pieces, shares, None)
    here, there = add_cores(give, keep, 3)
    sum_in, there = lax.optimization_barrier((sum_in, there))
    there = swap_dp(there, 2)
    r0, r2, r3 = add_rows(here, there)
    pieces = [pair(first), pair(fourth)]
    own_in, own_out, far_in, far_out, give, keep = expert(table, (1, 4), (), pieces, shares, (sum_in, sum_out))
    here, there = add_cores(give, keep, 2)
    there = swap_dp(there, 2)
    there, far_in, far_out = lax.optimization_barrier((there, far_in, far_out))
    r1, r4 = add_rows(here, there)
    far_in, far_out = swap_dp(far_in, 2), swap_dp(far_out, 2)
    total_in = own_in + far_in
    results = [r0] + [ahead(r, -o) for o, r in ((1, r1), (2, r2), (3, r3), (4, r4))]
    results[1], total_in = lax.optimization_barrier((results[1], total_in))
    done = merge(table, results, nblk)
    done, far_out = lax.optimization_barrier((done, far_out))
    return total_in[None], (own_out + far_out)[None], done.reshape(total, -1)


def solution(mesh):
    return jax.shard_map(
        on_device,
        mesh=mesh,
        in_specs=(
            P("blk", None),
            P("blk", None),
            P("blk", None, "dp", None),
            P("blk", "dp", None),
            P(),
        ),
        out_specs=(P("blk", None, "dp", None), P("blk", "dp", None), P("blk", "dp")),
        check_vma=False,
    )
```

```python
import functools

import jax
import jax.numpy as jnp
from jax import lax
from jax.experimental import pallas as pl
from jax.experimental.pallas import tpu as pltpu
from jax.sharding import PartitionSpec as P


HOPS = 4
SPAN = HOPS + 1
BLOCK = 128
MOST = 3
PARTS = 4
BF16 = jnp.bfloat16
F32 = jnp.float32


def size_of(axis):
    return lax.axis_size(axis)


def ahead(array, by, parity=None):
    size = size_of("blk")
    moves = lambda i: parity is None or i % 2 == parity
    return lax.ppermute(array, "blk", [((i + by) % size if moves(i) else i, i) for i in range(size)])


def swap_pair(array):
    return lax.ppermute(array, "blk", [(i, i ^ 1) for i in range(size_of("blk"))])


def swap_dp(array, bit):
    return lax.ppermute(array, "dp", [(i, i ^ bit) for i in range(size_of("dp"))])


def contract_last(lhs, rhs):
    return lax.dot_general(lhs, rhs, (((1,), (1,)), ((), ())), preferred_element_type=F32)


def matmul(lhs, rhs):
    return lax.dot_general(lhs, rhs, (((1,), (0,)), ((), ())), preferred_element_type=F32)


def whole(shape, **more):
    zeros = (0,) * len(shape)
    return pl.BlockSpec(tuple(shape), lambda i, s: zeros, **more)


OWN, ODD, WIN, START, LIM = 0, 1, 2, 2 + 2 * SPAN, 2 + 3 * SPAN
TABLE = LIM + SPAN * MOST


def table_kernel(n_dev, nblk, s_ref, out_ref):
    me, own = s_ref[0], s_ref[1]
    out_ref[OWN] = own
    out_ref[ODD] = lax.rem(me, 2)

    def count(device, o):
        return s_ref[2 + device * SPAN + o]

    def start(device, o):
        total = jnp.int32(0)
        for p in range(o):
            total += lax.div(count(device, p) + (BLOCK - 1), BLOCK)
        return total

    there = lax.rem(me + 2, n_dev)
    for o in range(SPAN):
        out_ref[START + o] = start(me, o)
        out_ref[WIN + o] = jnp.minimum(start(me, o), nblk - MOST)
        out_ref[WIN + SPAN + o] = jnp.minimum(start(there, o), nblk - MOST)
        device = lax.rem(me + o, n_dev)
        first = start(device, o)
        window = jnp.minimum(first, nblk - MOST)
        for t in range(MOST):
            block = window + t - first
            out_ref[LIM + o * MOST + t] = jnp.where(block >= 0, count(device, o) - block * BLOCK, 0)


def make_table(counts, n_dev, nblk):
    place = jnp.stack([lax.axis_index("blk"), lax.axis_index("dp")]).astype(jnp.int32)
    return pl.pallas_call(
        functools.partial(table_kernel, n_dev, nblk),
        out_shape=jax.ShapeDtypeStruct((TABLE,), jnp.int32),
        in_specs=[pl.BlockSpec(memory_space=pltpu.SMEM)],
        out_specs=pl.BlockSpec(memory_space=pltpu.SMEM),
    )(jnp.concatenate([place, counts.reshape(-1)]))


def cut(array, index):
    return lax.dynamic_slice_in_dim(array, index, MOST, 0)


def column(k, own):
    return (((k % 2) * 2) | (1 - k // 2)) ^ own


def expert_kernel(offsets, home, last, s_ref, *refs):
    refs = list(refs)
    take = lambda n: [refs.pop(0) for _ in range(n)]
    n_away = len(offsets) - home
    home_refs = take(2 * home)
    pieces = [take(2) for _ in range(n_away)]
    shares = take(4)
    add_in, add_out = take(2) if last else (None, None)
    if last:
        own_in, own_out, far_in, far_out = take(4)
    else:
        sum_in, sum_out = take(2)
    give, keep, w_ref, v_ref, sems, x_s, c_s, proj_s, hg_s, gu_s, gut_s, ht_s = refs
    step = pl.program_id(0)
    own = s_ref[OWN]
    core = own % 2
    half = BLOCK // 2
    quarter = BLOCK // PARTS
    depth = w_ref.shape[1]
    width = depth // PARTS
    units = v_ref.shape[0]
    fw = units // 2

    @pl.when(step == 0)
    def _():
        moves = []
        for k in range(2):
            w_share, v_share = shares[2 * k : 2 * k + 2]
            for g in range(2):
                moves.append((w_share.at[g], w_ref.at[pl.ds(g * units + k * fw, fw)]))
            moves.append((v_share, v_ref.at[pl.ds(k * fw, fw)]))
        for slot in range(len(offsets)):
            for t in range(MOST):
                base = (slot * MOST + t) * half
                if slot < home:
                    for ref, rows in zip(home_refs, (x_s, c_s)):
                        moves.append((ref.at[t, 0], rows.at[pl.ds(base, half)]))
                else:
                    for ref, at in zip(pieces[slot - home], (core, 1 - core)):
                        place = pl.ds(pl.multiple_of(base + at * quarter, quarter), quarter)
                        for g, rows in enumerate((x_s, c_s)):
                            moves.append((ref.at[t, g], rows.at[place]))
        copies = [pltpu.make_async_copy(a, b, sems.at[n]) for n, (a, b) in enumerate(moves)]
        for copy in copies:
            copy.start()
        for copy in copies:
            copy.wait()
        for slot in range(len(offsets)):
            for t in range(MOST):
                limit = s_ref[LIM + offsets[slot] * MOST + t]
                rows = pl.ds((slot * MOST + t) * half, half)

                @pl.when(limit < BLOCK)
                def _():
                    ids = lax.broadcasted_iota(jnp.int32, (half, 1), 0) + (own // 2) * half
                    c_s[rows, :] = jnp.where(ids < limit, c_s[rows, :], jnp.zeros((), BF16))

        proj_s[...] = contract_last(x_s[...], w_ref[...])
        hg_s[...] = contract_last(c_s[...], v_ref[...])
        gate_pre = proj_s[:, :units]
        up_pre = proj_s[:, units:]
        hidden_grad = hg_s[...]
        sig = jax.nn.sigmoid(gate_pre)
        active = gate_pre * sig
        hidden = (active * up_pre).astype(BF16)
        gate_rows = (hidden_grad * up_pre * sig * (1.0 + gate_pre * (1.0 - sig))).astype(BF16)
        up_rows = (hidden_grad * active).astype(BF16)
        gu_s[:, :units] = gate_rows
        gu_s[:, units:] = up_rows
        gut_s[:units, :] = gate_rows.T
        gut_s[units:, :] = up_rows.T
        ht_s[...] = hidden.T

    cols = pl.ds(pl.multiple_of(column(step, own) * width, width), width)
    new_in = matmul(gut_s[...], x_s[:, cols])
    new_out = matmul(ht_s[...], c_s[:, cols])
    if last:
        new_in += add_in[...]
        new_out += add_out[...]
        own_in[0] = new_in[:fw]
        own_in[1] = new_in[units : units + fw]
        own_out[...] = new_out[:fw]
        far_in[0] = new_in[fw:units].astype(BF16)
        far_in[1] = new_in[units + fw :].astype(BF16)
        far_out[...] = new_out[fw:].astype(BF16)
    else:
        sum_in[...] = new_in
        sum_out[...] = new_out
    row_grad = matmul(gu_s[...], w_ref[:, cols]).astype(BF16)

    @pl.when(step < 2)
    def _():
        give[0] = row_grad

    @pl.when(step >= 2)
    def _():
        keep[0] = row_grad


def expert(table, offsets, home, pieces, shares, sums):
    last = sums is not None
    fw, depth = shares[1].shape
    units = 2 * fw
    width = depth // PARTS
    half = BLOCK // 2
    rows = len(offsets) * MOST * half
    arrays, specs = [], []
    for a in home:
        arrays.append(a)
        specs.append(pl.BlockSpec(memory_space=pl.ANY))
    for pair in pieces:
        for a in pair:
            arrays.append(a)
            specs.append(pl.BlockSpec(memory_space=pl.ANY))
    for a in shares:
        arrays.append(a)
        specs.append(pl.BlockSpec(memory_space=pl.ANY))
    chunk_in = pl.BlockSpec((2 * units, width), lambda i, s: (0, column(i, s[OWN])))
    chunk_out = pl.BlockSpec((units, width), lambda i, s: (0, column(i, s[OWN])))
    own_in = pl.BlockSpec((2, fw, width), lambda i, s: (0, 0, column(i, s[OWN])))
    own_out = pl.BlockSpec((fw, width), lambda i, s: (0, column(i, s[OWN])))
    if last:
        arrays += list(sums)
        specs += [chunk_in, chunk_out]
        shapes = [((2, fw, depth), F32), ((fw, depth), F32), ((2, fw, depth), BF16), ((fw, depth), BF16)]
        outs = [own_in, own_out, own_in, own_out]
    else:
        shapes = [((2 * units, depth), F32), ((units, depth), F32)]
        outs = [chunk_in, chunk_out]
    shapes += [((2, rows, width), BF16)] * 2
    outs += [
        pl.BlockSpec((1, rows, width), lambda i, s: (jnp.minimum(i, 1), 0, 0)),
        pl.BlockSpec((1, rows, width), lambda i, s: (jnp.maximum(i - 2, 0), 0, 0)),
    ]
    return pl.pallas_call(
        functools.partial(expert_kernel, tuple(offsets), len(home) // 2, last),
        out_shape=[jax.ShapeDtypeStruct(*s) for s in shapes],
        grid_spec=pltpu.PrefetchScalarGridSpec(
            num_scalar_prefetch=1,
            grid=(PARTS,),
            in_specs=specs,
            out_specs=outs,
            scratch_shapes=[
                pltpu.VMEM((2 * units, depth), BF16),
                pltpu.VMEM((units, depth), BF16),
                pltpu.SemaphoreType.DMA((6 + MOST * (len(home) + 4 * len(pieces)),)),
                pltpu.VMEM((rows, depth), BF16),
                pltpu.VMEM((rows, depth), BF16),
                pltpu.VMEM((rows, 2 * units), F32),
                pltpu.VMEM((rows, units), F32),
                pltpu.VMEM((rows, 2 * units), BF16),
                pltpu.VMEM((2 * units, rows), BF16),
                pltpu.VMEM((units, rows), BF16),
            ],
        ),
        compiler_params=pltpu.CompilerParams(vmem_limit_bytes=25 * 2**20),
        cost_estimate=pl.CostEstimate(
            flops=16 * rows * units * depth,
            bytes_accessed=rows * depth * 6 + units * depth * (6 + (24 if last else 12)),
            transcendentals=rows * units,
        ),
    )(table, *arrays)


def add_cores(give, keep, n):
    got = swap_dp(give, 1)
    shape = (n, MOST, BLOCK // 2, keep.shape[-1])
    return [(keep[k].astype(F32) + got[k].astype(F32)).astype(BF16).reshape(shape) for k in range(2)]


def add_rows(here, other):
    return [jnp.stack([here[k], other[k]]) for k in range(other.shape[0])]


def merge_kernel(s_ref, *refs):
    *sources, out = refs
    half = BLOCK // 2
    y = s_ref[OWN] // 2
    for b in range(out.shape[0]):
        for o, source in enumerate(sources):
            begin = s_ref[START + o]
            end = s_ref[START + o + 1] if o + 1 < SPAN else out.shape[0]

            @pl.when((b >= begin) & (b < end))
            def _():
                at = jnp.clip(b - s_ref[WIN + o], 0, MOST - 1)
                out[b, pl.ds(pl.multiple_of(y * half, half), half), :] = source[0, at]
                out[b, pl.ds(pl.multiple_of((1 - y) * half, half), half), :] = source[1, at]


def merge(table, sources, nblk):
    shape = (nblk, BLOCK, sources[0].shape[-1])
    return pl.pallas_call(
        merge_kernel,
        out_shape=jax.ShapeDtypeStruct(shape, BF16),
        grid_spec=pltpu.PrefetchScalarGridSpec(
            num_scalar_prefetch=1,
            grid=(1,),
            in_specs=[whole(s.shape) for s in sources],
            out_specs=whole(shape),
        ),
    )(table, *sources)


def on_device(x_rows, grad_rows, w_gate_up, w_down, counts):
    w_in, w_out = w_gate_up[0], w_down[0]
    _, depth = w_out.shape
    total = x_rows.shape[0]
    nblk = total // BLOCK
    n_dev = size_of("blk")
    assert size_of("dp") == PARTS and n_dev % 2 == 0 and n_dev > HOPS
    part = BLOCK // PARTS
    own = lax.axis_index("dp")

    def pick(array, first, end):
        array = array.reshape(nblk, PARTS, part, depth)
        return lax.dynamic_slice(array, (first, own, 0, 0), (end - first, 1, part, depth))

    def quarter(first, end):
        return jnp.concatenate([pick(x_rows, first, end), pick(grad_rows, first, end)], axis=1)

    my_wide = quarter(MOST, nblk)
    wide = ahead(my_wide, 2)
    my_wide, counts, x_rows, grad_rows = lax.optimization_barrier((my_wide, counts, x_rows, grad_rows))
    my_narrow = quarter(1, MOST)
    narrow = ahead(my_narrow, 2)
    table = make_table(counts, n_dev, nblk)
    home = [
        lax.dynamic_slice(a.reshape(nblk, 2, -1, depth), (0, own // 2, 0, 0), (MOST, 1, BLOCK // 2, depth))
        for a in (x_rows, grad_rows)
    ]
    mine = quarter(1, nblk)
    mine = cut(mine, table[WIN + 1] - 1)
    o_in = swap_dp(w_in, 2)
    o_out = swap_dp(w_out, 2)

    third = cut(wide, table[WIN + SPAN + 3] - MOST)
    fourth = wide[nblk - 2 * MOST :]
    third = ahead(third, 1)
    fourth = ahead(fourth, 2)
    there = jnp.concatenate([narrow, wide])
    first = jnp.where(table[ODD] == 1, mine, cut(there, table[WIN + SPAN + 1] - 1))
    second = cut(there, table[WIN + SPAN + 2] - 1)
    first = swap_pair(first)

    def pair(a):
        return a, swap_dp(a, 1)

    shares = (w_in, w_out, o_in, o_out)
    pieces = [pair(second), pair(third)]
    sum_in, sum_out, give, keep = expert(table, (0, 2, 3), home, pieces, shares, None)
    here, there = add_cores(give, keep, 3)
    sum_in, there = lax.optimization_barrier((sum_in, there))
    there = swap_dp(there, 2)
    r0, r2, r3 = add_rows(here, there)
    pieces = [pair(first), pair(fourth)]
    own_in, own_out, far_in, far_out, give, keep = expert(table, (1, 4), (), pieces, shares, (sum_in, sum_out))
    far_out = swap_dp(far_out, 2)
    here, there = add_cores(give, keep, 2)
    there = swap_dp(there, 2)
    r1, r4 = add_rows(here, there)
    far_in = swap_dp(far_in, 2)
    r2, r3 = ahead(r2, -2), ahead(r3, -3)
    r1, r4 = ahead(r1, -1), ahead(r4, -4)
    done = merge(table, [r0, r1, r2, r3, r4], nblk)
    done, far_in = lax.optimization_barrier((done, far_in))
    return (own_in + far_in)[None], (own_out + far_out)[None], done.reshape(total, -1)


def solution(mesh):
    return jax.shard_map(
        on_device,
        mesh=mesh,
        in_specs=(
            P("blk", None),
            P("blk", None),
            P("blk", None, "dp", None),
            P("blk", "dp", None),
            P(),
        ),
        out_specs=(P("blk", None, "dp", None), P("blk", "dp", None), P("blk", "dp")),
        check_vma=False,
    )
```

```python
import functools

import jax
import jax.numpy as jnp
from jax import lax
from jax.experimental import pallas as pl
from jax.experimental.pallas import tpu as pltpu
from jax.sharding import PartitionSpec as P


HOPS = 4
SPAN = HOPS + 1
BLOCK = 128
MOST = 3
PARTS = 4
BF16 = jnp.bfloat16
F32 = jnp.float32


def size_of(axis):
    return lax.axis_size(axis)


def ahead(array, by, parity=None):
    size = size_of("blk")
    moves = lambda i: parity is None or i % 2 == parity
    return lax.ppermute(array, "blk", [((i + by) % size if moves(i) else i, i) for i in range(size)])


def ahead_even(array, by):
    size = size_of("blk")
    return lax.ppermute(array, "blk", [((i + by) % size, i) for i in range(0, size, 2)])


def swap_pair(array):
    return lax.ppermute(array, "blk", [(i, i ^ 1) for i in range(size_of("blk"))])


def swap_dp(array, bit):
    return lax.ppermute(array, "dp", [(i, i ^ bit) for i in range(size_of("dp"))])


def contract_last(lhs, rhs):
    return lax.dot_general(lhs, rhs, (((1,), (1,)), ((), ())), preferred_element_type=F32)


def matmul(lhs, rhs):
    return lax.dot_general(lhs, rhs, (((1,), (0,)), ((), ())), preferred_element_type=F32)


def whole(shape, **more):
    zeros = (0,) * len(shape)
    return pl.BlockSpec(tuple(shape), lambda i, s: zeros, **more)


OWN, ODD, WIN, START, LIM = 0, 1, 2, 2 + 2 * SPAN, 2 + 3 * SPAN
TABLE = LIM + SPAN * MOST


def table_kernel(n_dev, nblk, s_ref, out_ref):
    me, own = s_ref[0], s_ref[1]
    out_ref[OWN] = own
    out_ref[ODD] = lax.rem(me, 2)

    def count(device, o):
        return s_ref[2 + device * SPAN + o]

    def start(device, o):
        total = jnp.int32(0)
        for p in range(o):
            total += lax.div(count(device, p) + (BLOCK - 1), BLOCK)
        return total

    there = lax.rem(me + 2, n_dev)
    for o in range(SPAN):
        out_ref[START + o] = start(me, o)
        out_ref[WIN + o] = jnp.minimum(start(me, o), nblk - MOST)
        out_ref[WIN + SPAN + o] = jnp.minimum(start(there, o), nblk - MOST)
        device = lax.rem(me + o, n_dev)
        first = start(device, o)
        window = jnp.minimum(first, nblk - MOST)
        for t in range(MOST):
            block = window + t - first
            out_ref[LIM + o * MOST + t] = jnp.where(block >= 0, count(device, o) - block * BLOCK, 0)


def make_table(counts, n_dev, nblk):
    place = jnp.stack([lax.axis_index("blk"), lax.axis_index("dp")]).astype(jnp.int32)
    return pl.pallas_call(
        functools.partial(table_kernel, n_dev, nblk),
        out_shape=jax.ShapeDtypeStruct((TABLE,), jnp.int32),
        in_specs=[pl.BlockSpec(memory_space=pltpu.SMEM)],
        out_specs=pl.BlockSpec(memory_space=pltpu.SMEM),
    )(jnp.concatenate([place, counts.reshape(-1)]))


def cut(array, index):
    return lax.dynamic_slice_in_dim(array, index, MOST, 0)


def column(k, own):
    return (((k % 2) * 2) | (1 - k // 2)) ^ own


def expert_kernel(offsets, home, last, s_ref, *refs):
    refs = list(refs)
    take = lambda n: [refs.pop(0) for _ in range(n)]
    n_away = len(offsets) - home
    home_refs = take(2 * home)
    pieces = [take(2) for _ in range(n_away)]
    shares = take(4)
    add_in, add_out = take(2) if last else (None, None)
    if last:
        own_in, own_out, far_in, far_out = take(4)
    else:
        sum_in, sum_out = take(2)
    give, keep, w_ref, v_ref, sems, x_s, c_s, proj_s, hg_s, gu_s, gut_s, ht_s = refs
    step = pl.program_id(0)
    own = s_ref[OWN]
    core = own % 2
    half = BLOCK // 2
    quarter = BLOCK // PARTS
    depth = w_ref.shape[1]
    width = depth // PARTS
    units = v_ref.shape[0]
    fw = units // 2

    @pl.when(step == 0)
    def _():
        moves = []
        for k in range(2):
            w_share, v_share = shares[2 * k : 2 * k + 2]
            for g in range(2):
                moves.append((w_share.at[g], w_ref.at[pl.ds(g * units + k * fw, fw)]))
            moves.append((v_share, v_ref.at[pl.ds(k * fw, fw)]))
        copies = [pltpu.make_async_copy(a, b, sems.at[n]) for n, (a, b) in enumerate(moves)]
        for copy in copies:
            copy.start()

        def put(slot, t, at, x, c):
            size = x.shape[0]
            rows = pl.ds(pl.multiple_of((slot * MOST + t) * half + at, quarter), size)
            ids = lax.broadcasted_iota(jnp.int32, (size, 1), 0) + (own // 2) * half + at
            live = ids < s_ref[LIM + offsets[slot] * MOST + t]
            x_s[rows, :] = x
            c_s[rows, :] = jnp.where(live, c, jnp.zeros((), BF16))

        for slot in range(len(offsets)):
            for t in range(MOST):
                if slot < home:
                    put(slot, t, 0, home_refs[0][t, 0], home_refs[1][t, 0])
                else:
                    near, other = pieces[slot - home]
                    put(slot, t, core * quarter, near[t, 0], near[t, 1])
                    put(slot, t, (1 - core) * quarter, other[t, 0], other[t, 1])
        for copy in copies:
            copy.wait()
        proj_s[...] = contract_last(x_s[...], w_ref[...])
        hg_s[...] = contract_last(c_s[...], v_ref[...])
        gate_pre = proj_s[:, :units]
        up_pre = proj_s[:, units:]
        hidden_grad = hg_s[...]
        sig = jax.nn.sigmoid(gate_pre)
        active = gate_pre * sig
        hidden = (active * up_pre).astype(BF16)
        gate_rows = (hidden_grad * up_pre * sig * (1.0 + gate_pre * (1.0 - sig))).astype(BF16)
        up_rows = (hidden_grad * active).astype(BF16)
        gu_s[:, :units] = gate_rows
        gu_s[:, units:] = up_rows
        gut_s[:units, :] = gate_rows.T
        gut_s[units:, :] = up_rows.T
        ht_s[...] = hidden.T

    cols = pl.ds(pl.multiple_of(column(step, own) * width, width), width)
    new_in = matmul(gut_s[...], x_s[:, cols])
    new_out = matmul(ht_s[...], c_s[:, cols])
    if last:
        new_in += add_in[...]
        new_out += add_out[...]
        own_in[0] = new_in[:fw]
        own_in[1] = new_in[units : units + fw]
        own_out[...] = new_out[:fw]
        far_in[0] = new_in[fw:units].astype(BF16)
        far_in[1] = new_in[units + fw :].astype(BF16)
        far_out[...] = new_out[fw:].astype(BF16)
    else:
        sum_in[...] = new_in
        sum_out[...] = new_out
    row_grad = matmul(gu_s[...], w_ref[:, cols]).astype(BF16)

    @pl.when(step < 2)
    def _():
        give[0] = row_grad

    @pl.when(step >= 2)
    def _():
        keep[0] = row_grad


def expert(table, offsets, home, pieces, shares, sums):
    last = sums is not None
    fw, depth = shares[1].shape
    units = 2 * fw
    width = depth // PARTS
    half = BLOCK // 2
    rows = len(offsets) * MOST * half
    arrays, specs = [], []
    once = pl.Buffered(1)
    for a in list(home) + [a for pair in pieces for a in pair]:
        arrays.append(a)
        specs.append(whole(a.shape, pipeline_mode=once))
    for a in shares:
        arrays.append(a)
        specs.append(pl.BlockSpec(memory_space=pl.ANY))
    chunk_in = pl.BlockSpec((2 * units, width), lambda i, s: (0, column(i, s[OWN])))
    chunk_out = pl.BlockSpec((units, width), lambda i, s: (0, column(i, s[OWN])))
    own_in = pl.BlockSpec((2, fw, width), lambda i, s: (0, 0, column(i, s[OWN])))
    own_out = pl.BlockSpec((fw, width), lambda i, s: (0, column(i, s[OWN])))
    if last:
        arrays += list(sums)
        specs += [chunk_in, chunk_out]
        shapes = [((2, fw, depth), F32), ((fw, depth), F32), ((2, fw, depth), BF16), ((fw, depth), BF16)]
        outs = [own_in, own_out, own_in, own_out]
    else:
        shapes = [((2 * units, depth), F32), ((units, depth), F32)]
        outs = [chunk_in, chunk_out]
    shapes += [((2, rows, width), BF16)] * 2
    outs += [
        pl.BlockSpec((1, rows, width), lambda i, s: (jnp.minimum(i, 1), 0, 0)),
        pl.BlockSpec((1, rows, width), lambda i, s: (jnp.maximum(i - 2, 0), 0, 0)),
    ]
    return pl.pallas_call(
        functools.partial(expert_kernel, tuple(offsets), len(home) // 2, last),
        out_shape=[jax.ShapeDtypeStruct(*s) for s in shapes],
        grid_spec=pltpu.PrefetchScalarGridSpec(
            num_scalar_prefetch=1,
            grid=(PARTS,),
            in_specs=specs,
            out_specs=outs,
            scratch_shapes=[
                pltpu.VMEM((2 * units, depth), BF16),
                pltpu.VMEM((units, depth), BF16),
                pltpu.SemaphoreType.DMA((6,)),
                pltpu.VMEM((rows, depth), BF16),
                pltpu.VMEM((rows, depth), BF16),
                pltpu.VMEM((rows, 2 * units), F32),
                pltpu.VMEM((rows, units), F32),
                pltpu.VMEM((rows, 2 * units), BF16),
                pltpu.VMEM((2 * units, rows), BF16),
                pltpu.VMEM((units, rows), BF16),
            ],
        ),
        compiler_params=pltpu.CompilerParams(vmem_limit_bytes=28 * 2**20),
        cost_estimate=pl.CostEstimate(
            flops=16 * rows * units * depth,
            bytes_accessed=rows * depth * 6 + units * depth * (6 + (24 if last else 12)),
            transcendentals=rows * units,
        ),
    )(table, *arrays)


def add_cores(give, keep, n):
    got = swap_dp(give, 1)
    shape = (n, MOST, BLOCK // 2, keep.shape[-1])
    return [(keep[k].astype(F32) + got[k].astype(F32)).astype(BF16).reshape(shape) for k in range(2)]


def add_rows(here, other):
    return [jnp.stack([here[k], other[k]]) for k in range(other.shape[0])]


def merge_kernel(s_ref, *refs):
    *sources, out = refs
    half = BLOCK // 2
    y = s_ref[OWN] // 2
    for b in range(out.shape[0]):
        for o, source in enumerate(sources):
            begin = s_ref[START + o]
            end = s_ref[START + o + 1] if o + 1 < SPAN else out.shape[0]

            @pl.when((b >= begin) & (b < end))
            def _():
                at = jnp.clip(b - s_ref[WIN + o], 0, MOST - 1)
                out[b, pl.ds(pl.multiple_of(y * half, half), half), :] = source[0, at]
                out[b, pl.ds(pl.multiple_of((1 - y) * half, half), half), :] = source[1, at]


def merge(table, sources, nblk):
    shape = (nblk, BLOCK, sources[0].shape[-1])
    return pl.pallas_call(
        merge_kernel,
        out_shape=jax.ShapeDtypeStruct(shape, BF16),
        grid_spec=pltpu.PrefetchScalarGridSpec(
            num_scalar_prefetch=1,
            grid=(1,),
            in_specs=[whole(s.shape) for s in sources],
            out_specs=whole(shape),
        ),
    )(table, *sources)


def on_device(x_rows, grad_rows, w_gate_up, w_down, counts):
    w_in, w_out = w_gate_up[0], w_down[0]
    _, depth = w_out.shape
    total = x_rows.shape[0]
    nblk = total // BLOCK
    n_dev = size_of("blk")
    assert size_of("dp") == PARTS and n_dev % 2 == 0 and n_dev > HOPS
    part = BLOCK // PARTS
    own = lax.axis_index("dp")

    def pick(array, first, end):
        array = array.reshape(nblk, PARTS, part, depth)
        return lax.dynamic_slice(array, (first, own, 0, 0), (end - first, 1, part, depth))

    def quarter(first, end):
        return jnp.concatenate([pick(x_rows, first, end), pick(grad_rows, first, end)], axis=1)

    my_wide = quarter(MOST, nblk)
    wide = ahead(my_wide, 2)
    my_wide, counts, x_rows, grad_rows = lax.optimization_barrier((my_wide, counts, x_rows, grad_rows))
    my_two, my_one = quarter(2, MOST), quarter(1, 2)
    two = ahead(my_two, 2)
    one = ahead_even(my_one, 2)
    table = make_table(counts, n_dev, nblk)
    home = [
        lax.dynamic_slice(a.reshape(nblk, 2, -1, depth), (0, own // 2, 0, 0), (MOST, 1, BLOCK // 2, depth))
        for a in (x_rows, grad_rows)
    ]
    mine = quarter(1, nblk)
    mine = cut(mine, table[WIN + 1] - 1)
    o_in = swap_dp(w_in, 2)
    o_out = swap_dp(w_out, 2)

    third = cut(wide, table[WIN + SPAN + 3] - MOST)
    fourth = wide[nblk - 2 * MOST :]
    third = ahead(third, 1)
    fourth = ahead(fourth, 2)
    there = jnp.concatenate([one, two, wide])
    first = jnp.where(table[ODD] == 1, mine, cut(there, table[WIN + SPAN + 1] - 1))
    second = cut(there, table[WIN + SPAN + 2] - 1)
    first = swap_pair(first)

    def pair(a):
        return a, swap_dp(a, 1)

    shares = (w_in, w_out, o_in, o_out)
    pieces = [pair(second), pair(third)]
    sum_in, sum_out, give, keep = expert(table, (0, 2, 3), home, pieces, shares, None)
    here, there = add_cores(give, keep, 3)
    sum_in, there = lax.optimization_barrier((sum_in, there))
    there = swap_dp(there, 2)
    r0, r2, r3 = add_rows(here, there)
    pieces = [pair(first), pair(fourth)]
    own_in, own_out, far_in, far_out, give, keep = expert(table, (1, 4), (), pieces, shares, (sum_in, sum_out))
    far_out = swap_dp(far_out, 2)
    here, there = add_cores(give, keep, 2)
    there = swap_dp(there, 2)
    r1, r4 = add_rows(here, there)
    far_in = swap_dp(far_in, 2)
    r2, r3 = ahead(r2, -2), ahead(r3, -3)
    r1, r4 = ahead(r1, -1), ahead(r4, -4)
    done = merge(table, [r0, r1, r2, r3, r4], nblk)
    done, far_in = lax.optimization_barrier((done, far_in))
    return (own_in + far_in)[None], (own_out + far_out)[None], done.reshape(total, -1)


def solution(mesh):
    return jax.shard_map(
        on_device,
        mesh=mesh,
        in_specs=(
            P("blk", None),
            P("blk", None),
            P("blk", None, "dp", None),
            P("blk", "dp", None),
            P(),
        ),
        out_specs=(P("blk", None, "dp", None), P("blk", "dp", None), P("blk", "dp")),
        check_vma=False,
    )
```

```python
import functools

import jax
import jax.numpy as jnp
from jax import lax
from jax.experimental import pallas as pl
from jax.experimental.pallas import tpu as pltpu
from jax.sharding import PartitionSpec as P


HOPS = 4
SPAN = HOPS + 1
BLOCK = 128
MOST = 3
PARTS = 4
BF16 = jnp.bfloat16
F32 = jnp.float32


def size_of(axis):
    return lax.axis_size(axis)


def ahead(array, by, parity=None):
    size = size_of("blk")
    moves = lambda i: parity is None or i % 2 == parity
    return lax.ppermute(array, "blk", [((i + by) % size if moves(i) else i, i) for i in range(size)])


def ahead_even(array, by):
    size = size_of("blk")
    return lax.ppermute(array, "blk", [((i + by) % size, i) for i in range(0, size, 2)])


def swap_pair(array):
    return lax.ppermute(array, "blk", [(i, i ^ 1) for i in range(size_of("blk"))])


def swap_dp(array, bit):
    return lax.ppermute(array, "dp", [(i, i ^ bit) for i in range(size_of("dp"))])


def contract_last(lhs, rhs):
    return lax.dot_general(lhs, rhs, (((1,), (1,)), ((), ())), preferred_element_type=F32)


def matmul(lhs, rhs):
    return lax.dot_general(lhs, rhs, (((1,), (0,)), ((), ())), preferred_element_type=F32)


def whole(shape, **more):
    zeros = (0,) * len(shape)
    return pl.BlockSpec(tuple(shape), lambda i, s: zeros, **more)


OWN, ODD, WIN, START, LIM = 0, 1, 2, 2 + 2 * SPAN, 2 + 3 * SPAN
TABLE = LIM + SPAN * MOST


def table_kernel(n_dev, nblk, s_ref, out_ref):
    me, own = s_ref[0], s_ref[1]
    out_ref[OWN] = own
    out_ref[ODD] = lax.rem(me, 2)

    def count(device, o):
        return s_ref[2 + device * SPAN + o]

    def start(device, o):
        total = jnp.int32(0)
        for p in range(o):
            total += lax.div(count(device, p) + (BLOCK - 1), BLOCK)
        return total

    there = lax.rem(me + 2, n_dev)
    for o in range(SPAN):
        out_ref[START + o] = start(me, o)
        out_ref[WIN + o] = jnp.minimum(start(me, o), nblk - MOST)
        out_ref[WIN + SPAN + o] = jnp.minimum(start(there, o), nblk - MOST)
        device = lax.rem(me + o, n_dev)
        first = start(device, o)
        window = jnp.minimum(first, nblk - MOST)
        for t in range(MOST):
            block = window + t - first
            out_ref[LIM + o * MOST + t] = jnp.where(block >= 0, count(device, o) - block * BLOCK, 0)


def make_table(counts, n_dev, nblk):
    place = jnp.stack([lax.axis_index("blk"), lax.axis_index("dp")]).astype(jnp.int32)
    return pl.pallas_call(
        functools.partial(table_kernel, n_dev, nblk),
        out_shape=jax.ShapeDtypeStruct((TABLE,), jnp.int32),
        in_specs=[pl.BlockSpec(memory_space=pltpu.SMEM)],
        out_specs=pl.BlockSpec(memory_space=pltpu.SMEM),
    )(jnp.concatenate([place, counts.reshape(-1)]))


def cut(array, index):
    return lax.dynamic_slice_in_dim(array, index, MOST, 0)


def column(k, own):
    return (((k % 2) * 2) | (1 - k // 2)) ^ own


def expert_kernel(offsets, home, last, s_ref, *refs):
    refs = list(refs)
    take = lambda n: [refs.pop(0) for _ in range(n)]
    n_away = len(offsets) - home
    home_refs = take(2 * home)
    pieces = [take(2) for _ in range(n_away)]
    shares = take(4)
    add_in, add_out = take(2) if last else (None, None)
    if last:
        own_in, own_out, far_gate, far_up, far_out = take(5)
    else:
        sum_in, sum_out = take(2)
    give, keep, w_ref, v_ref, sems, x_s, c_s, proj_s, hg_s, gu_s, gut_s, ht_s = refs
    step = pl.program_id(0)
    own = s_ref[OWN]
    core = own % 2
    half = BLOCK // 2
    quarter = BLOCK // PARTS
    depth = w_ref.shape[1]
    width = depth // PARTS
    units = v_ref.shape[0]
    fw = units // 2

    @pl.when(step == 0)
    def _():
        moves = []
        for k in range(2):
            w_share, v_share = shares[2 * k : 2 * k + 2]
            for g in range(2):
                moves.append((w_share.at[g], w_ref.at[pl.ds(g * units + k * fw, fw)]))
            moves.append((v_share, v_ref.at[pl.ds(k * fw, fw)]))
        copies = [pltpu.make_async_copy(a, b, sems.at[n]) for n, (a, b) in enumerate(moves)]
        for copy in copies:
            copy.start()

        def put(slot, t, at, x, c):
            size = x.shape[0]
            rows = pl.ds(pl.multiple_of((slot * MOST + t) * half + at, quarter), size)
            ids = lax.broadcasted_iota(jnp.int32, (size, 1), 0) + (own // 2) * half + at
            live = ids < s_ref[LIM + offsets[slot] * MOST + t]
            x_s[rows, :] = x
            c_s[rows, :] = jnp.where(live, c, jnp.zeros((), BF16))

        for slot in range(len(offsets)):
            for t in range(MOST):
                if slot < home:
                    put(slot, t, 0, home_refs[0][t, 0], home_refs[1][t, 0])
                else:
                    near, other = pieces[slot - home]
                    put(slot, t, core * quarter, near[t, 0], near[t, 1])
                    put(slot, t, (1 - core) * quarter, other[t, 0], other[t, 1])
        for copy in copies:
            copy.wait()
        proj_s[...] = contract_last(x_s[...], w_ref[...])
        hg_s[...] = contract_last(c_s[...], v_ref[...])
        gate_pre = proj_s[:, :units]
        up_pre = proj_s[:, units:]
        hidden_grad = hg_s[...]
        sig = jax.nn.sigmoid(gate_pre)
        active = gate_pre * sig
        hidden = (active * up_pre).astype(BF16)
        gate_rows = (hidden_grad * up_pre * sig * (1.0 + gate_pre * (1.0 - sig))).astype(BF16)
        up_rows = (hidden_grad * active).astype(BF16)
        gu_s[:, :units] = gate_rows
        gu_s[:, units:] = up_rows
        gut_s[:units, :] = gate_rows.T
        gut_s[units:, :] = up_rows.T
        ht_s[...] = hidden.T

    cols = pl.ds(pl.multiple_of(column(step, own) * width, width), width)
    new_in = matmul(gut_s[...], x_s[:, cols])
    new_out = matmul(ht_s[...], c_s[:, cols])
    if last:
        new_in += add_in[...]
        new_out += add_out[...]
        own_in[0] = new_in[:fw]
        own_in[1] = new_in[units : units + fw]
        own_out[...] = new_out[:fw]
        far_gate[...] = new_in[fw:units].astype(BF16)
        far_up[...] = new_in[units + fw :].astype(BF16)
        far_out[...] = new_out[fw:].astype(BF16)
    else:
        sum_in[...] = new_in
        sum_out[...] = new_out
    row_grad = matmul(gu_s[...], w_ref[:, cols]).astype(BF16)

    @pl.when(step < 2)
    def _():
        give[0] = row_grad

    @pl.when(step >= 2)
    def _():
        keep[0] = row_grad


def expert(table, offsets, home, pieces, shares, sums):
    last = sums is not None
    fw, depth = shares[1].shape
    units = 2 * fw
    width = depth // PARTS
    half = BLOCK // 2
    rows = len(offsets) * MOST * half
    arrays, specs = [], []
    once = pl.Buffered(1)
    for a in list(home) + [a for pair in pieces for a in pair]:
        arrays.append(a)
        specs.append(whole(a.shape, pipeline_mode=once))
    for a in shares:
        arrays.append(a)
        specs.append(pl.BlockSpec(memory_space=pl.ANY))
    chunk_in = pl.BlockSpec((2 * units, width), lambda i, s: (0, column(i, s[OWN])))
    chunk_out = pl.BlockSpec((units, width), lambda i, s: (0, column(i, s[OWN])))
    own_in = pl.BlockSpec((2, fw, width), lambda i, s: (0, 0, column(i, s[OWN])))
    own_out = pl.BlockSpec((fw, width), lambda i, s: (0, column(i, s[OWN])))
    if last:
        arrays += list(sums)
        specs += [chunk_in, chunk_out]
        shapes = [((2, fw, depth), F32), ((fw, depth), F32)] + [((fw, depth), BF16)] * 3
        outs = [own_in] + [own_out] * 4
    else:
        shapes = [((2 * units, depth), F32), ((units, depth), F32)]
        outs = [chunk_in, chunk_out]
    shapes += [((2, rows, width), BF16)] * 2
    outs += [
        pl.BlockSpec((1, rows, width), lambda i, s: (jnp.minimum(i, 1), 0, 0)),
        pl.BlockSpec((1, rows, width), lambda i, s: (jnp.maximum(i - 2, 0), 0, 0)),
    ]
    return pl.pallas_call(
        functools.partial(expert_kernel, tuple(offsets), len(home) // 2, last),
        out_shape=[jax.ShapeDtypeStruct(*s) for s in shapes],
        grid_spec=pltpu.PrefetchScalarGridSpec(
            num_scalar_prefetch=1,
            grid=(PARTS,),
            in_specs=specs,
            out_specs=outs,
            scratch_shapes=[
                pltpu.VMEM((2 * units, depth), BF16),
                pltpu.VMEM((units, depth), BF16),
                pltpu.SemaphoreType.DMA((6,)),
                pltpu.VMEM((rows, depth), BF16),
                pltpu.VMEM((rows, depth), BF16),
                pltpu.VMEM((rows, 2 * units), F32),
                pltpu.VMEM((rows, units), F32),
                pltpu.VMEM((rows, 2 * units), BF16),
                pltpu.VMEM((2 * units, rows), BF16),
                pltpu.VMEM((units, rows), BF16),
            ],
        ),
        compiler_params=pltpu.CompilerParams(vmem_limit_bytes=28 * 2**20),
        cost_estimate=pl.CostEstimate(
            flops=16 * rows * units * depth,
            bytes_accessed=rows * depth * 6 + units * depth * (6 + (24 if last else 12)),
            transcendentals=rows * units,
        ),
    )(table, *arrays)


def add_cores(give, keep, n):
    got = swap_dp(give, 1)
    shape = (n, MOST, BLOCK // 2, keep.shape[-1])
    return [(keep[k].astype(F32) + got[k].astype(F32)).astype(BF16).reshape(shape) for k in range(2)]


def add_rows(here, other):
    return [jnp.stack([here[k], other[k]]) for k in range(other.shape[0])]


def merge_kernel(s_ref, *refs):
    *sources, out = refs
    half = BLOCK // 2
    y = s_ref[OWN] // 2
    for b in range(out.shape[0]):
        for o, source in enumerate(sources):
            begin = s_ref[START + o]
            end = s_ref[START + o + 1] if o + 1 < SPAN else out.shape[0]

            @pl.when((b >= begin) & (b < end))
            def _():
                at = jnp.clip(b - s_ref[WIN + o], 0, MOST - 1)
                out[b, pl.ds(pl.multiple_of(y * half, half), half), :] = source[0, at]
                out[b, pl.ds(pl.multiple_of((1 - y) * half, half), half), :] = source[1, at]


def merge(table, sources, nblk):
    shape = (nblk, BLOCK, sources[0].shape[-1])
    return pl.pallas_call(
        merge_kernel,
        out_shape=jax.ShapeDtypeStruct(shape, BF16),
        grid_spec=pltpu.PrefetchScalarGridSpec(
            num_scalar_prefetch=1,
            grid=(1,),
            in_specs=[whole(s.shape) for s in sources],
            out_specs=whole(shape),
        ),
    )(table, *sources)


def on_device(x_rows, grad_rows, w_gate_up, w_down, counts):
    w_in, w_out = w_gate_up[0], w_down[0]
    _, depth = w_out.shape
    total = x_rows.shape[0]
    nblk = total // BLOCK
    n_dev = size_of("blk")
    assert size_of("dp") == PARTS and n_dev % 2 == 0 and n_dev > HOPS
    part = BLOCK // PARTS
    own = lax.axis_index("dp")

    def pick(array, first, end):
        array = array.reshape(nblk, PARTS, part, depth)
        return lax.dynamic_slice(array, (first, own, 0, 0), (end - first, 1, part, depth))

    def quarter(first, end):
        return jnp.concatenate([pick(x_rows, first, end), pick(grad_rows, first, end)], axis=1)

    my_wide = quarter(MOST, nblk)
    wide = ahead(my_wide, 2)
    my_wide, counts, x_rows, grad_rows = lax.optimization_barrier((my_wide, counts, x_rows, grad_rows))
    my_two, my_one = quarter(2, MOST), quarter(1, 2)
    two = ahead(my_two, 2)
    one = ahead_even(my_one, 2)
    table = make_table(counts, n_dev, nblk)
    home = [
        lax.dynamic_slice(a.reshape(nblk, 2, -1, depth), (0, own // 2, 0, 0), (MOST, 1, BLOCK // 2, depth))
        for a in (x_rows, grad_rows)
    ]
    mine = quarter(1, nblk)
    mine = cut(mine, table[WIN + 1] - 1)
    o_in = swap_dp(w_in, 2)
    o_out = swap_dp(w_out, 2)

    third = cut(wide, table[WIN + SPAN + 3] - MOST)
    fourth = wide[nblk - 2 * MOST :]
    third = ahead(third, 1)
    fourth = ahead(fourth, 2)
    there = jnp.concatenate([one, two, wide])
    first = jnp.where(table[ODD] == 1, mine, cut(there, table[WIN + SPAN + 1] - 1))
    second = cut(there, table[WIN + SPAN + 2] - 1)
    first = swap_pair(first)

    def pair(a):
        return a, swap_dp(a, 1)

    shares = (w_in, w_out, o_in, o_out)
    pieces = [pair(second), pair(third)]
    sum_in, sum_out, give, keep = expert(table, (0, 2, 3), home, pieces, shares, None)
    here, there = add_cores(give, keep, 3)
    sum_in, there = lax.optimization_barrier((sum_in, there))
    there = swap_dp(there, 2)
    r0, r2, r3 = add_rows(here, there)
    pieces = [pair(first), pair(fourth)]
    own_in, own_out, far_gate, far_up, far_out, give, keep = expert(table, (1, 4), (), pieces, shares, (sum_in, sum_out))
    far_gate = swap_dp(far_gate, 2)
    here, there = add_cores(give, keep, 2)
    there = swap_dp(there, 2)
    r1, r4 = add_rows(here, there)
    far_up = swap_dp(far_up, 2)
    far_out = swap_dp(far_out, 2)
    r2, r3 = ahead(r2, -2), ahead(r3, -3)
    r1, r4 = ahead(r1, -1), ahead(r4, -4)
    done = merge(table, [r0, r1, r2, r3, r4], nblk)
    total_in = own_in + jnp.stack([far_gate, far_up])
    total_in, done, far_out = lax.optimization_barrier((total_in, done, far_out))
    return total_in[None], (own_out + far_out)[None], done.reshape(total, -1)


def solution(mesh):
    return jax.shard_map(
        on_device,
        mesh=mesh,
        in_specs=(
            P("blk", None),
            P("blk", None),
            P("blk", None, "dp", None),
            P("blk", "dp", None),
            P(),
        ),
        out_specs=(P("blk", None, "dp", None), P("blk", "dp", None), P("blk", "dp")),
        check_vma=False,
    )
```

```python
import functools

import jax
import jax.numpy as jnp
from jax import lax
from jax.experimental import pallas as pl
from jax.experimental.pallas import tpu as pltpu
from jax.sharding import PartitionSpec as P


HOPS = 4
SPAN = HOPS + 1
BLOCK = 128
MOST = 3
PARTS = 4
BF16 = jnp.bfloat16
F32 = jnp.float32


def size_of(axis):
    return lax.axis_size(axis)


def ahead(array, by, parity=None):
    size = size_of("blk")
    moves = lambda i: parity is None or i % 2 == parity
    return lax.ppermute(array, "blk", [((i + by) % size if moves(i) else i, i) for i in range(size)])


def ahead_even(array, by):
    size = size_of("blk")
    return lax.ppermute(array, "blk", [((i + by) % size, i) for i in range(0, size, 2)])


def swap_pair(array):
    return lax.ppermute(array, "blk", [(i, i ^ 1) for i in range(size_of("blk"))])


def swap_dp(array, bit):
    return lax.ppermute(array, "dp", [(i, i ^ bit) for i in range(size_of("dp"))])


def contract_last(lhs, rhs):
    return lax.dot_general(lhs, rhs, (((1,), (1,)), ((), ())), preferred_element_type=F32)


def matmul(lhs, rhs):
    return lax.dot_general(lhs, rhs, (((1,), (0,)), ((), ())), preferred_element_type=F32)


def whole(shape, **more):
    zeros = (0,) * len(shape)
    return pl.BlockSpec(tuple(shape), lambda i, s: zeros, **more)


OWN, ODD, WIN, START, LIM = 0, 1, 2, 2 + 2 * SPAN, 2 + 3 * SPAN
TABLE = LIM + SPAN * MOST


def table_kernel(n_dev, nblk, s_ref, out_ref):
    me, own = s_ref[0], s_ref[1]
    out_ref[OWN] = own
    out_ref[ODD] = lax.rem(me, 2)

    def count(device, o):
        return s_ref[2 + device * SPAN + o]

    def start(device, o):
        total = jnp.int32(0)
        for p in range(o):
            total += lax.div(count(device, p) + (BLOCK - 1), BLOCK)
        return total

    there = lax.rem(me + 2, n_dev)
    for o in range(SPAN):
        out_ref[START + o] = start(me, o)
        out_ref[WIN + o] = jnp.minimum(start(me, o), nblk - MOST)
        out_ref[WIN + SPAN + o] = jnp.minimum(start(there, o), nblk - MOST)
        device = lax.rem(me + o, n_dev)
        first = start(device, o)
        window = jnp.minimum(first, nblk - MOST)
        for t in range(MOST):
            block = window + t - first
            out_ref[LIM + o * MOST + t] = jnp.where(block >= 0, count(device, o) - block * BLOCK, 0)


def make_table(counts, n_dev, nblk):
    place = jnp.stack([lax.axis_index("blk"), lax.axis_index("dp")]).astype(jnp.int32)
    return pl.pallas_call(
        functools.partial(table_kernel, n_dev, nblk),
        out_shape=jax.ShapeDtypeStruct((TABLE,), jnp.int32),
        in_specs=[pl.BlockSpec(memory_space=pltpu.SMEM)],
        out_specs=pl.BlockSpec(memory_space=pltpu.SMEM),
    )(jnp.concatenate([place, counts.reshape(-1)]))


def cut(array, index):
    return lax.dynamic_slice_in_dim(array, index, MOST, 0)


def column(k, own):
    return (((k % 2) * 2) | (1 - k // 2)) ^ own


def expert_kernel(offsets, home, last, far_half, s_ref, *refs):
    refs = list(refs)
    take = lambda n: [refs.pop(0) for _ in range(n)]
    n_away = len(offsets) - home
    home_refs = take(2 * home)
    pieces = [take(2) for _ in range(n_away)]
    shares = take(4)
    add_in, add_out = take(2) if last else (None, None)
    if last:
        own_in, own_out, far_gate, far_up, far_out = take(5)
    elif not far_half:
        sum_in, sum_out = take(2)
    give, keep, w_ref, v_ref, sems, x_s, c_s, proj_s, hg_s, gu_s, gut_s, ht_s = refs
    step = pl.program_id(0)
    own = s_ref[OWN]
    core = own % 2
    half = BLOCK // 2
    quarter = BLOCK // PARTS
    depth = w_ref.shape[1]
    width = depth // PARTS
    units = v_ref.shape[0]
    fw = units // 2
    side = own // 2 ^ 1 if far_half else own // 2

    @pl.when(step == 0)
    def _():
        moves = []
        for k in range(2):
            w_share, v_share = shares[2 * k : 2 * k + 2]
            for g in range(2):
                moves.append((w_share.at[g], w_ref.at[pl.ds(g * units + k * fw, fw)]))
            moves.append((v_share, v_ref.at[pl.ds(k * fw, fw)]))
        copies = [pltpu.make_async_copy(a, b, sems.at[n]) for n, (a, b) in enumerate(moves)]
        for copy in copies:
            copy.start()

        def put(slot, t, at, x, c):
            size = x.shape[0]
            rows = pl.ds(pl.multiple_of((slot * MOST + t) * half + at, quarter), size)
            ids = lax.broadcasted_iota(jnp.int32, (size, 1), 0) + side * half + at
            live = ids < s_ref[LIM + offsets[slot] * MOST + t]
            x_s[rows, :] = x
            c_s[rows, :] = jnp.where(live, c, jnp.zeros((), BF16))

        for slot in range(len(offsets)):
            for t in range(MOST):
                if slot < home:
                    put(slot, t, 0, home_refs[0][t, 0], home_refs[1][t, 0])
                else:
                    near, other = pieces[slot - home]
                    put(slot, t, core * quarter, near[t, 0], near[t, 1])
                    put(slot, t, (1 - core) * quarter, other[t, 0], other[t, 1])
        for copy in copies:
            copy.wait()
        proj_s[...] = contract_last(x_s[...], w_ref[...])
        hg_s[...] = contract_last(c_s[...], v_ref[...])
        gate_pre = proj_s[:, :units]
        up_pre = proj_s[:, units:]
        hidden_grad = hg_s[...]
        sig = jax.nn.sigmoid(gate_pre)
        active = gate_pre * sig
        hidden = (active * up_pre).astype(BF16)
        gate_rows = (hidden_grad * up_pre * sig * (1.0 + gate_pre * (1.0 - sig))).astype(BF16)
        up_rows = (hidden_grad * active).astype(BF16)
        gu_s[:, :units] = gate_rows
        gu_s[:, units:] = up_rows
        if not far_half:
            gut_s[:units, :] = gate_rows.T
            gut_s[units:, :] = up_rows.T
            ht_s[...] = hidden.T

    cols = pl.ds(pl.multiple_of(column(step, own) * width, width), width)
    if not far_half:
        new_in = matmul(gut_s[...], x_s[:, cols])
        new_out = matmul(ht_s[...], c_s[:, cols])
    if last:
        new_in += add_in[...]
        new_out += add_out[...]
        own_in[0] = new_in[:fw]
        own_in[1] = new_in[units : units + fw]
        own_out[...] = new_out[:fw]
        far_gate[...] = new_in[fw:units].astype(BF16)
        far_up[...] = new_in[units + fw :].astype(BF16)
        far_out[...] = new_out[fw:].astype(BF16)
    elif not far_half:
        sum_in[...] = new_in
        sum_out[...] = new_out
    row_grad = matmul(gu_s[...], w_ref[:, cols]).astype(BF16)

    @pl.when(step < 2)
    def _():
        give[0] = row_grad

    @pl.when(step >= 2)
    def _():
        keep[0] = row_grad


def expert(table, offsets, home, pieces, shares, sums=None, far_half=False):
    last = sums is not None
    fw, depth = shares[1].shape
    units = 2 * fw
    width = depth // PARTS
    half = BLOCK // 2
    rows = len(offsets) * MOST * half
    arrays, specs = [], []
    once = pl.Buffered(1)
    for a in list(home) + [a for pair in pieces for a in pair]:
        arrays.append(a)
        specs.append(whole(a.shape, pipeline_mode=once))
    for a in shares:
        arrays.append(a)
        specs.append(pl.BlockSpec(memory_space=pl.ANY))
    chunk_in = pl.BlockSpec((2 * units, width), lambda i, s: (0, column(i, s[OWN])))
    chunk_out = pl.BlockSpec((units, width), lambda i, s: (0, column(i, s[OWN])))
    own_in = pl.BlockSpec((2, fw, width), lambda i, s: (0, 0, column(i, s[OWN])))
    own_out = pl.BlockSpec((fw, width), lambda i, s: (0, column(i, s[OWN])))
    if last:
        arrays += list(sums)
        specs += [chunk_in, chunk_out]
        shapes = [((2, fw, depth), F32), ((fw, depth), F32)] + [((fw, depth), BF16)] * 3
        outs = [own_in] + [own_out] * 4
    elif far_half:
        shapes, outs = [], []
    else:
        shapes = [((2 * units, depth), F32), ((units, depth), F32)]
        outs = [chunk_in, chunk_out]
    shapes += [((2, rows, width), BF16)] * 2
    outs += [
        pl.BlockSpec((1, rows, width), lambda i, s: (jnp.minimum(i, 1), 0, 0)),
        pl.BlockSpec((1, rows, width), lambda i, s: (jnp.maximum(i - 2, 0), 0, 0)),
    ]
    return pl.pallas_call(
        functools.partial(expert_kernel, tuple(offsets), len(home) // 2, last, far_half),
        out_shape=[jax.ShapeDtypeStruct(*s) for s in shapes],
        grid_spec=pltpu.PrefetchScalarGridSpec(
            num_scalar_prefetch=1,
            grid=(PARTS,),
            in_specs=specs,
            out_specs=outs,
            scratch_shapes=[
                pltpu.VMEM((2 * units, depth), BF16),
                pltpu.VMEM((units, depth), BF16),
                pltpu.SemaphoreType.DMA((6,)),
                pltpu.VMEM((rows, depth), BF16),
                pltpu.VMEM((rows, depth), BF16),
                pltpu.VMEM((rows, 2 * units), F32),
                pltpu.VMEM((rows, units), F32),
                pltpu.VMEM((rows, 2 * units), BF16),
                pltpu.VMEM((2 * units, rows), BF16),
                pltpu.VMEM((units, rows), BF16),
            ],
        ),
        compiler_params=pltpu.CompilerParams(vmem_limit_bytes=25 * 2**20),
        cost_estimate=pl.CostEstimate(
            flops=16 * rows * units * depth,
            bytes_accessed=rows * depth * 6 + units * depth * (6 + (24 if last else 12)),
            transcendentals=rows * units,
        ),
    )(table, *arrays)


def add_cores(give, keep, n):
    got = swap_dp(give, 1)
    shape = (n, MOST, BLOCK // 2, keep.shape[-1])
    return [(keep[k].astype(F32) + got[k].astype(F32)).astype(BF16).reshape(shape) for k in range(2)]


def add_rows(here, other):
    return [jnp.stack([here[k], other[k]]) for k in range(other.shape[0])]


def merge_kernel(s_ref, *refs):
    *sources, out = refs
    half = BLOCK // 2
    y = s_ref[OWN] // 2
    for b in range(out.shape[0]):
        for o, source in enumerate(sources):
            begin = s_ref[START + o]
            end = s_ref[START + o + 1] if o + 1 < SPAN else out.shape[0]

            @pl.when((b >= begin) & (b < end))
            def _():
                at = jnp.clip(b - s_ref[WIN + o], 0, MOST - 1)
                out[b, pl.ds(pl.multiple_of(y * half, half), half), :] = source[0, at]
                out[b, pl.ds(pl.multiple_of((1 - y) * half, half), half), :] = source[1, at]


def merge(table, sources, nblk):
    shape = (nblk, BLOCK, sources[0].shape[-1])
    return pl.pallas_call(
        merge_kernel,
        out_shape=jax.ShapeDtypeStruct(shape, BF16),
        grid_spec=pltpu.PrefetchScalarGridSpec(
            num_scalar_prefetch=1,
            grid=(1,),
            in_specs=[whole(s.shape) for s in sources],
            out_specs=whole(shape),
        ),
    )(table, *sources)


def on_device(x_rows, grad_rows, w_gate_up, w_down, counts):
    w_in, w_out = w_gate_up[0], w_down[0]
    _, depth = w_out.shape
    total = x_rows.shape[0]
    nblk = total // BLOCK
    n_dev = size_of("blk")
    assert size_of("dp") == PARTS and n_dev % 2 == 0 and n_dev > HOPS
    part = BLOCK // PARTS
    own = lax.axis_index("dp")

    def pick(array, first, end):
        array = array.reshape(nblk, PARTS, part, depth)
        return lax.dynamic_slice(array, (first, own, 0, 0), (end - first, 1, part, depth))

    def quarter(first, end):
        return jnp.concatenate([pick(x_rows, first, end), pick(grad_rows, first, end)], axis=1)

    my_wide = quarter(MOST, nblk)
    wide = ahead(my_wide, 2)
    my_wide, counts, x_rows, grad_rows = lax.optimization_barrier((my_wide, counts, x_rows, grad_rows))
    my_two, my_one = quarter(2, MOST), quarter(1, 2)
    two = ahead(my_two, 2)
    one = ahead_even(my_one, 2)
    table = make_table(counts, n_dev, nblk)
    home = [
        [
            lax.dynamic_slice(a.reshape(nblk, 2, -1, depth), (0, side, 0, 0), (MOST, 1, BLOCK // 2, depth))
            for a in (x_rows, grad_rows)
        ]
        for side in (own // 2, 1 - own // 2)
    ]
    mine = quarter(1, nblk)
    mine = cut(mine, table[WIN + 1] - 1)
    o_in = swap_dp(w_in, 2)
    o_out = swap_dp(w_out, 2)

    third = cut(wide, table[WIN + SPAN + 3] - MOST)
    fourth = wide[nblk - 2 * MOST :]
    third = ahead(third, 1)
    fourth = ahead(fourth, 2)
    there = jnp.concatenate([one, two, wide])
    first = jnp.where(table[ODD] == 1, mine, cut(there, table[WIN + SPAN + 1] - 1))
    second = cut(there, table[WIN + SPAN + 2] - 1)
    first = swap_pair(first)

    def pair(a):
        return a, swap_dp(a, 1)

    shares = (w_in, w_out, o_in, o_out)
    pieces = [pair(second), pair(third)]
    sum_in, sum_out, give, keep = expert(table, (0, 2, 3), home[0], pieces, shares)
    here_early, there = add_cores(give, keep, 3)
    sum_in, there = lax.optimization_barrier((sum_in, there[1:]))
    there = swap_dp(there, 2)
    r2, r3 = add_rows(here_early[1:], there)
    pieces = [pair(first), pair(fourth)]
    own_in, own_out, far_gate, far_up, far_out, give, keep = expert(table, (1, 4), (), pieces, shares, (sum_in, sum_out))
    far_gate = swap_dp(far_gate, 2)
    here, there = add_cores(give, keep, 2)
    there = swap_dp(there, 2)
    r1, r4 = add_rows(here, there)
    far_up = swap_dp(far_up, 2)
    far_out = swap_dp(far_out, 2)
    give, keep = expert(table, (0,), home[1], [], shares, far_half=True)
    got = swap_dp(give[0], 1)
    other = (keep[0].astype(F32) + got.astype(F32)).astype(BF16).reshape(here_early[0].shape)
    r0 = jnp.stack([here_early[0], other])
    r2, r3 = ahead(r2, -2), ahead(r3, -3)
    r1, r4 = ahead(r1, -1), ahead(r4, -4)
    done = merge(table, [r0, r1, r2, r3, r4], nblk)
    total_in = own_in + jnp.stack([far_gate, far_up])
    total_in, done, far_out = lax.optimization_barrier((total_in, done, far_out))
    return total_in[None], (own_out + far_out)[None], done.reshape(total, -1)


def solution(mesh):
    return jax.shard_map(
        on_device,
        mesh=mesh,
        in_specs=(
            P("blk", None),
            P("blk", None),
            P("blk", None, "dp", None),
            P("blk", "dp", None),
            P(),
        ),
        out_specs=(P("blk", None, "dp", None), P("blk", "dp", None), P("blk", "dp")),
        check_vma=False,
    )
```

```python
import functools

import jax
import jax.numpy as jnp
from jax import lax
from jax.experimental import pallas as pl
from jax.experimental.pallas import tpu as pltpu
from jax.sharding import PartitionSpec as P


HOPS = 4
SPAN = HOPS + 1
BLOCK = 128
MOST = 3
PARTS = 4
BF16 = jnp.bfloat16
F32 = jnp.float32


def size_of(axis):
    return lax.axis_size(axis)


def ahead(array, by, parity=None):
    size = size_of("blk")
    moves = lambda i: parity is None or i % 2 == parity
    return lax.ppermute(array, "blk", [((i + by) % size if moves(i) else i, i) for i in range(size)])


def ahead_even(array, by):
    size = size_of("blk")
    return lax.ppermute(array, "blk", [((i + by) % size, i) for i in range(0, size, 2)])


def swap_pair(array):
    return lax.ppermute(array, "blk", [(i, i ^ 1) for i in range(size_of("blk"))])


def swap_dp(array, bit):
    return lax.ppermute(array, "dp", [(i, i ^ bit) for i in range(size_of("dp"))])


def contract_last(lhs, rhs):
    return lax.dot_general(lhs, rhs, (((1,), (1,)), ((), ())), preferred_element_type=F32)


def matmul(lhs, rhs):
    return lax.dot_general(lhs, rhs, (((1,), (0,)), ((), ())), preferred_element_type=F32)


def whole(shape, **more):
    zeros = (0,) * len(shape)
    return pl.BlockSpec(tuple(shape), lambda i, s: zeros, **more)


OWN, ODD, WIN, START, LIM = 0, 1, 2, 2 + 2 * SPAN, 2 + 3 * SPAN
TABLE = LIM + SPAN * MOST


def table_kernel(n_dev, nblk, s_ref, out_ref):
    me, own = s_ref[0], s_ref[1]
    out_ref[OWN] = own
    out_ref[ODD] = lax.rem(me, 2)

    def count(device, o):
        return s_ref[2 + device * SPAN + o]

    def start(device, o):
        total = jnp.int32(0)
        for p in range(o):
            total += lax.div(count(device, p) + (BLOCK - 1), BLOCK)
        return total

    there = lax.rem(me + 2, n_dev)
    for o in range(SPAN):
        out_ref[START + o] = start(me, o)
        out_ref[WIN + o] = jnp.minimum(start(me, o), nblk - MOST)
        out_ref[WIN + SPAN + o] = jnp.minimum(start(there, o), nblk - MOST)
        device = lax.rem(me + o, n_dev)
        first = start(device, o)
        window = jnp.minimum(first, nblk - MOST)
        for t in range(MOST):
            block = window + t - first
            out_ref[LIM + o * MOST + t] = jnp.where(block >= 0, count(device, o) - block * BLOCK, 0)


def make_table(counts, n_dev, nblk):
    place = jnp.stack([lax.axis_index("blk"), lax.axis_index("dp")]).astype(jnp.int32)
    return pl.pallas_call(
        functools.partial(table_kernel, n_dev, nblk),
        out_shape=jax.ShapeDtypeStruct((TABLE,), jnp.int32),
        in_specs=[pl.BlockSpec(memory_space=pltpu.SMEM)],
        out_specs=pl.BlockSpec(memory_space=pltpu.SMEM),
    )(jnp.concatenate([place, counts.reshape(-1)]))


def cut(array, index):
    return lax.dynamic_slice_in_dim(array, index, MOST, 0)


def column(k, own):
    return (((k % 2) * 2) | (1 - k // 2)) ^ own


def expert_kernel(offsets, home, last, s_ref, *refs):
    refs = list(refs)
    take = lambda n: [refs.pop(0) for _ in range(n)]
    n_away = len(offsets) - home
    home_refs = take(2 * home)
    pieces = [take(2) for _ in range(n_away)]
    shares = take(4)
    add_in, add_out = take(2) if last else (None, None)
    if last:
        own_in, own_out, far_gate, far_up, far_out = take(5)
    else:
        sum_in, sum_out = take(2)
    give, keep, w_ref, v_ref, sems, x_s, c_s, proj_s, hg_s, gu_s, gut_s, ht_s = refs
    step = pl.program_id(0)
    own = s_ref[OWN]
    core = own % 2
    half = BLOCK // 2
    quarter = BLOCK // PARTS
    depth = w_ref.shape[1]
    width = depth // PARTS
    units = v_ref.shape[0]
    fw = units // 2

    @pl.when(step == 0)
    def _():
        moves = []
        for k in range(2):
            w_share, v_share = shares[2 * k : 2 * k + 2]
            for g in range(2):
                moves.append((w_share.at[g], w_ref.at[pl.ds(g * units + k * fw, fw)]))
            moves.append((v_share, v_ref.at[pl.ds(k * fw, fw)]))
        copies = [pltpu.make_async_copy(a, b, sems.at[n]) for n, (a, b) in enumerate(moves)]
        for copy in copies:
            copy.start()

        def put(slot, t, at, x, c):
            size = x.shape[0]
            rows = pl.ds(pl.multiple_of((slot * MOST + t) * half + at, quarter), size)
            ids = lax.broadcasted_iota(jnp.int32, (size, 1), 0) + (own // 2) * half + at
            live = ids < s_ref[LIM + offsets[slot] * MOST + t]
            x_s[rows, :] = x
            c_s[rows, :] = jnp.where(live, c, jnp.zeros((), BF16))

        for slot in range(len(offsets)):
            for t in range(MOST):
                if slot < home:
                    put(slot, t, 0, home_refs[0][t, 0], home_refs[1][t, 0])
                else:
                    near, other = pieces[slot - home]
                    put(slot, t, core * quarter, near[t, 0], near[t, 1])
                    put(slot, t, (1 - core) * quarter, other[t, 0], other[t, 1])
        for copy in copies:
            copy.wait()
        proj_s[...] = contract_last(x_s[...], w_ref[...])
        hg_s[...] = contract_last(c_s[...], v_ref[...])
        gate_pre = proj_s[:, :units]
        up_pre = proj_s[:, units:]
        hidden_grad = hg_s[...]
        sig = jax.nn.sigmoid(gate_pre)
        active = gate_pre * sig
        hidden = (active * up_pre).astype(BF16)
        gate_rows = (hidden_grad * up_pre * sig * (1.0 + gate_pre * (1.0 - sig))).astype(BF16)
        up_rows = (hidden_grad * active).astype(BF16)
        gu_s[:, :units] = gate_rows
        gu_s[:, units:] = up_rows
        gut_s[:units, :] = gate_rows.T
        gut_s[units:, :] = up_rows.T
        ht_s[...] = hidden.T

    cols = pl.ds(pl.multiple_of(column(step, own) * width, width), width)
    new_in = matmul(gut_s[...], x_s[:, cols])
    new_out = matmul(ht_s[...], c_s[:, cols])
    if last:
        new_in += add_in[...]
        new_out += add_out[...]
        own_in[0] = new_in[:fw]
        own_in[1] = new_in[units : units + fw]
        own_out[...] = new_out[:fw]
        far_gate[...] = new_in[fw:units].astype(BF16)
        far_up[...] = new_in[units + fw :].astype(BF16)
        far_out[...] = new_out[fw:].astype(BF16)
    else:
        sum_in[...] = new_in
        sum_out[...] = new_out
    row_grad = matmul(gu_s[...], w_ref[:, cols]).astype(BF16)

    @pl.when(step < 2)
    def _():
        give[0] = row_grad

    @pl.when(step >= 2)
    def _():
        keep[0] = row_grad


def expert(table, offsets, home, pieces, shares, sums):
    last = sums is not None
    fw, depth = shares[1].shape
    units = 2 * fw
    width = depth // PARTS
    half = BLOCK // 2
    rows = len(offsets) * MOST * half
    arrays, specs = [], []
    once = pl.Buffered(1)
    for a in list(home) + [a for pair in pieces for a in pair]:
        arrays.append(a)
        specs.append(whole(a.shape, pipeline_mode=once))
    for a in shares:
        arrays.append(a)
        specs.append(pl.BlockSpec(memory_space=pl.ANY))
    chunk_in = pl.BlockSpec((2 * units, width), lambda i, s: (0, column(i, s[OWN])))
    chunk_out = pl.BlockSpec((units, width), lambda i, s: (0, column(i, s[OWN])))
    own_in = pl.BlockSpec((2, fw, width), lambda i, s: (0, 0, column(i, s[OWN])))
    own_out = pl.BlockSpec((fw, width), lambda i, s: (0, column(i, s[OWN])))
    if last:
        arrays += list(sums)
        specs += [chunk_in, chunk_out]
        shapes = [((2, fw, depth), F32), ((fw, depth), F32)] + [((fw, depth), BF16)] * 3
        outs = [own_in] + [own_out] * 4
    else:
        shapes = [((2 * units, depth), F32), ((units, depth), F32)]
        outs = [chunk_in, chunk_out]
    shapes += [((2, rows, width), BF16)] * 2
    outs += [
        pl.BlockSpec((1, rows, width), lambda i, s: (jnp.minimum(i, 1), 0, 0)),
        pl.BlockSpec((1, rows, width), lambda i, s: (jnp.maximum(i - 2, 0), 0, 0)),
    ]
    return pl.pallas_call(
        functools.partial(expert_kernel, tuple(offsets), len(home) // 2, last),
        out_shape=[jax.ShapeDtypeStruct(*s) for s in shapes],
        grid_spec=pltpu.PrefetchScalarGridSpec(
            num_scalar_prefetch=1,
            grid=(PARTS,),
            in_specs=specs,
            out_specs=outs,
            scratch_shapes=[
                pltpu.VMEM((2 * units, depth), BF16),
                pltpu.VMEM((units, depth), BF16),
                pltpu.SemaphoreType.DMA((6,)),
                pltpu.VMEM((rows, depth), BF16),
                pltpu.VMEM((rows, depth), BF16),
                pltpu.VMEM((rows, 2 * units), F32),
                pltpu.VMEM((rows, units), F32),
                pltpu.VMEM((rows, 2 * units), BF16),
                pltpu.VMEM((2 * units, rows), BF16),
                pltpu.VMEM((units, rows), BF16),
            ],
        ),
        compiler_params=pltpu.CompilerParams(vmem_limit_bytes=28 * 2**20),
        cost_estimate=pl.CostEstimate(
            flops=16 * rows * units * depth,
            bytes_accessed=rows * depth * 6 + units * depth * (6 + (24 if last else 12)),
            transcendentals=rows * units,
        ),
    )(table, *arrays)


def add_cores(give, keep, n):
    got = swap_dp(give, 1)
    shape = (n, MOST, BLOCK // 2, keep.shape[-1])
    return [(keep[k].astype(F32) + got[k].astype(F32)).astype(BF16).reshape(shape) for k in range(2)]


def add_rows(here, other):
    return [jnp.stack([here[k], other[k]]) for k in range(other.shape[0])]


def merge_kernel(s_ref, *refs):
    *sources, out = refs
    half = BLOCK // 2
    y = s_ref[OWN] // 2
    for b in range(out.shape[0]):
        for o, source in enumerate(sources):
            begin = s_ref[START + o]
            end = s_ref[START + o + 1] if o + 1 < SPAN else out.shape[0]

            @pl.when((b >= begin) & (b < end))
            def _():
                at = jnp.clip(b - s_ref[WIN + o], 0, MOST - 1)
                out[b, pl.ds(pl.multiple_of(y * half, half), half), :] = source[0, at]
                out[b, pl.ds(pl.multiple_of((1 - y) * half, half), half), :] = source[1, at]


def merge(table, sources, nblk):
    shape = (nblk, BLOCK, sources[0].shape[-1])
    return pl.pallas_call(
        merge_kernel,
        out_shape=jax.ShapeDtypeStruct(shape, BF16),
        grid_spec=pltpu.PrefetchScalarGridSpec(
            num_scalar_prefetch=1,
            grid=(1,),
            in_specs=[whole(s.shape) for s in sources],
            out_specs=whole(shape),
        ),
    )(table, *sources)


def on_device(x_rows, grad_rows, w_gate_up, w_down, counts):
    w_in, w_out = w_gate_up[0], w_down[0]
    _, depth = w_out.shape
    total = x_rows.shape[0]
    nblk = total // BLOCK
    n_dev = size_of("blk")
    assert size_of("dp") == PARTS and n_dev % 2 == 0 and n_dev > HOPS
    part = BLOCK // PARTS
    own = lax.axis_index("dp")

    def pick(array, first, end):
        array = array.reshape(nblk, PARTS, part, depth)
        return lax.dynamic_slice(array, (first, own, 0, 0), (end - first, 1, part, depth))

    def quarter(first, end):
        return jnp.concatenate([pick(x_rows, first, end), pick(grad_rows, first, end)], axis=1)

    my_x, my_c = pick(x_rows, MOST, nblk), pick(grad_rows, MOST, nblk)
    wide_x = ahead(my_x, 2)
    wide_c = ahead(my_c, 2)
    my_x, my_c, counts, x_rows, grad_rows = lax.optimization_barrier((my_x, my_c, counts, x_rows, grad_rows))
    my_two, my_one = quarter(2, MOST), quarter(1, 2)
    two = ahead(my_two, 2)
    one = ahead_even(my_one, 2)
    table = make_table(counts, n_dev, nblk)
    home = [
        lax.dynamic_slice(a.reshape(nblk, 2, -1, depth), (0, own // 2, 0, 0), (MOST, 1, BLOCK // 2, depth))
        for a in (x_rows, grad_rows)
    ]
    mine = quarter(1, nblk)
    mine = cut(mine, table[WIN + 1] - 1)
    o_in = swap_dp(w_in, 2)
    o_out = swap_dp(w_out, 2)

    begin = table[WIN + SPAN + 3] - MOST
    third_x, fourth_x = cut(wide_x, begin), wide_x[nblk - 2 * MOST :]
    third = jnp.concatenate([third_x, cut(wide_c, begin)], axis=1)
    fourth = jnp.concatenate([fourth_x, wide_c[nblk - 2 * MOST :]], axis=1)
    third = ahead(third, 1)
    fourth = ahead(fourth, 2)
    there = jnp.concatenate([one, two, jnp.concatenate([wide_x, wide_c], axis=1)])
    first = jnp.where(table[ODD] == 1, mine, cut(there, table[WIN + SPAN + 1] - 1))
    second = cut(there, table[WIN + SPAN + 2] - 1)
    first = swap_pair(first)

    def pair(a):
        return a, swap_dp(a, 1)

    shares = (w_in, w_out, o_in, o_out)
    pieces = [pair(second), pair(third)]
    sum_in, sum_out, give, keep = expert(table, (0, 2, 3), home, pieces, shares, None)
    here, there = add_cores(give, keep, 3)
    sum_in, there = lax.optimization_barrier((sum_in, there))
    there = swap_dp(there, 2)
    r0, r2, r3 = add_rows(here, there)
    pieces = [pair(first), pair(fourth)]
    own_in, own_out, far_gate, far_up, far_out, give, keep = expert(table, (1, 4), (), pieces, shares, (sum_in, sum_out))
    far_gate = swap_dp(far_gate, 2)
    here, there = add_cores(give, keep, 2)
    there = swap_dp(there, 2)
    r1, r4 = add_rows(here, there)
    far_up = swap_dp(far_up, 2)
    far_out = swap_dp(far_out, 2)
    r2, r3 = ahead(r2, -2), ahead(r3, -3)
    r1, r4 = ahead(r1, -1), ahead(r4, -4)
    done = merge(table, [r0, r1, r2, r3, r4], nblk)
    total_in = own_in + jnp.stack([far_gate, far_up])
    total_in, done, far_out = lax.optimization_barrier((total_in, done, far_out))
    return total_in[None], (own_out + far_out)[None], done.reshape(total, -1)


def solution(mesh):
    return jax.shard_map(
        on_device,
        mesh=mesh,
        in_specs=(
            P("blk", None),
            P("blk", None),
            P("blk", None, "dp", None),
            P("blk", "dp", None),
            P(),
        ),
        out_specs=(P("blk", None, "dp", None), P("blk", "dp", None), P("blk", "dp")),
        check_vma=False,
    )
```
